32 devices in a mesh: groups: 2 (over y), seq: 4 (over z), head: 4 (over x, core).
Axes of the slice: x: 2, y: 2, z: 4, core: 2. Of those that a mesh axis runs over, the one named last changes fastest.
Arguments:
- layer_queries: bfloat16 [4096, 4096], P(('groups', 'seq'), 'head'), parts along dimension 0, may hold values from -1.75 to 1.75
- layer_keys: bfloat16 [4096, 4096], P(('groups', 'seq'), 'head'), parts along dimension 0, may hold values from -1.75 to 1.75
- layer_values: bfloat16 [4096, 4096], P(('groups', 'seq'), 'head'), parts along dimension 0, may hold values from -6 to 6
- gate_logits: bfloat16 [4096, 4096], P(('groups', 'seq'), 'head'), parts along dimension 0, may hold values from -6 to 6
- norm_gain: bfloat16 [4096], P('head'), may hold values from 0.099609375 to 1.8984375
- decay_exponents: int32 [32], P('head'), may hold values from 0 to 9
- doc_lengths: int32 [8], P('groups'), parts along dimension 0, may hold values from 1 to 1024, 2048 in all
- out_weight: bfloat16 [6144, 4096], P('seq', 'head'), may hold values from -0.125 to 0.125
Outputs:
- layer_output: bfloat16 [4096, 6144], P(('groups', 'seq'), 'head'), parts along dimension 0
The draws below stay inside these ranges and needn't reach their ends.
There are 2 independent parts, one for each index of `groups`. The reference program is written for one: setup_inputs(seed, part) draws one part's arguments, and reference() takes and returns one part's arrays. A program takes and returns all parts, laid end to end along the dimension named above; an argument that names none is the same for every part. Nothing has to cross between parts.
Inputs may be any that keep to these rules, and one draw needn't show every extreme that they name: `doc_lengths`: the lengths sum to 2048.
All inputs are finite; a program needn't handle non-finite values.
Results may differ from the reference program's by a relative error of at most 0.0063.
Values may be sent and summed in bfloat16 or wider, within the bound.
No kernel may reach another device: no remote copies, remote signals or barrier semaphores. Data moves between devices by JAX's collectives and lax.ppermute only.
A program may use at most 128 MiB of HBM per device.

```python
import math
import jax
import jax.numpy as jnp
import numpy as np
from jax import lax

D = 6144
HEAD_DIM = 128
HEADS = 32
TOK_DEV = 512
DOCS = 4
TOKENS = 2048
N_SEQ = 4


def draw_decay_exponents(key, part):
    first_key, second_key, third_key, fourth_key = jax.random.split(key, 4)
    picker = jax.random.randint(first_key, (HEADS,), 0, 2)
    slower = jax.random.randint(second_key, (HEADS,), 0, 2)
    faster = jax.random.randint(third_key, (HEADS,), 6, 10)
    chosen = picker * slower + (1 - picker) * faster
    shuffled = jax.random.permutation(fourth_key, HEADS)
    chosen = chosen.at[shuffled[0]].set(0).at[shuffled[1]].set(9)
    return chosen.astype(jnp.int32)


def spiked(values, stream_key, source, target, parts, factor):
    def block_of(dim):
        return (jnp.arange(values.shape[dim]) // (values.shape[dim] // parts)).reshape((-1,) + (1,) * (values.ndim - 1 - dim))

    first = jax.random.permutation(stream_key, parts)[block_of(target)]
    second = (block_of(target) + parts // 2) % parts
    return jnp.where((block_of(source) == first) | (block_of(source) == second), factor * values, values)


def levels(own_key, dims, pieces, smallest, top_value):
    level, own = 1.0, jax.random.fold_in(own_key, 6)
    for dim, blocks in pieces:
        draws = jnp.exp(jax.random.uniform(jax.random.fold_in(own, dim), (blocks,), jnp.float32, smallest / len(pieces), top_value / len(pieces)))
        level = level * jnp.repeat(draws, dims[dim] // blocks).reshape([-1 if axis == dim else 1 for axis in range(len(dims))])
    return level


def split_up(amount, total, most, slope):
    loads = [(1 << 20) // math.isqrt(rank ** slope) + 1 for rank in range(2, amount + 1)]
    rest, counts = total - most - (amount - 1), [1] * (amount - 1)
    while rest > 0:
        free = [i for i in range(amount - 1) if counts[i] < most]
        whole, left = sum([loads[i] for i in free]), rest
        for i in free:
            addition = min(most - counts[i], max(1, left * loads[i] // whole), rest)
            counts[i] = counts[i] + addition
            rest = rest - addition
    return np.array([most] + counts)


def uneven(own_key, count, total, limit, skew):
    if count == 2:
        one = jax.random.randint(own_key, (), max(1, total - limit), min(limit, total - 1) + 1)
        return jnp.stack([one, total - one])
    tallies = jnp.asarray(split_up(count, total, limit, skew), jnp.int32)
    couples = (count - 1) // 2
    giver, receiver = tallies[1:1 + 2 * couples:2], tallies[2:2 + 2 * couples:2]
    slack = jnp.minimum(giver - 1, limit - receiver)
    moved = jax.random.randint(jax.random.fold_in(own_key, 1), (couples,), 0, 1 << 20) % (slack + 1)
    tallies = tallies.at[1:1 + 2 * couples:2].set(giver - moved).at[2:2 + 2 * couples:2].set(receiver + moved)
    return tallies[jax.random.permutation(jax.random.fold_in(own_key, 2), count)]


def gaussian(own_key, extent, scale, bound, cuts=(), kind=jnp.bfloat16):
    drawn = jax.random.normal(own_key, extent, jnp.float32) * scale
    if len(cuts) > 0:
        drawn = levels(own_key, extent, cuts, -0.22, 0.18) * drawn
    return jnp.clip(drawn, min=-bound, max=bound).astype(kind)


def bell_draw_with(key, dims, width, limit, pieces, heavy, kind=jnp.bfloat16):
    array = width * jax.random.normal(key, dims, jnp.float32)
    if pieces:
        array = array * levels(key, dims, pieces, -0.22, 0.18)
    return jnp.clip(spiked(array, jax.random.fold_in(key, 3), *heavy), -limit, limit).astype(kind)


def setup_inputs(seed: int = 0, part: int = 0) -> dict:
    keys = jax.random.split(jax.random.key(seed), 9)
    own_keys = jax.random.split(jax.random.fold_in(keys[8], part), 9)
    layer_queries = gaussian(own_keys[0], (TOKENS, HEADS * HEAD_DIM), 0.3, 1.75, ((0, 4), (1, 4)))
    layer_keys = gaussian(own_keys[1], (TOKENS, HEADS * HEAD_DIM), 0.3, 1.75, ((0, 4), (1, 4)))
    layer_values = gaussian(own_keys[2], (TOKENS, HEADS * HEAD_DIM), 1.0, 6.0, ((0, 4), (1, 4)))
    gate_logits = gaussian(own_keys[3], (TOKENS, HEADS * HEAD_DIM), 1.0, 6.0, ((0, 4), (1, 4)))
    norm_gain = jnp.clip(1.0 + 0.18 * jax.random.normal(keys[4], (HEADS * HEAD_DIM,), jnp.float32), 0.099609375, 1.8984375).astype(jnp.bfloat16)
    decay_exponents = draw_decay_exponents(jax.random.fold_in(keys[8], 71), part)
    doc_lengths = uneven(own_keys[6], DOCS, TOKENS, TOKENS // 2, 0).astype(jnp.int32)
    out_weight = bell_draw_with(keys[7], (D, HEADS * HEAD_DIM), (HEADS * HEAD_DIM) ** -0.5, 0.125, ((0, 4), (1, 4)), (1, 0, 4, 2.0))
    return {"layer_queries": layer_queries, "layer_keys": layer_keys, "layer_values": layer_values, "gate_logits": gate_logits, "norm_gain": norm_gain, "decay_exponents": decay_exponents, "doc_lengths": doc_lengths, "out_weight": out_weight}


def doc_positions(doc_lengths, first_row, count):
    position = first_row + jnp.arange(count, dtype=jnp.int32)
    starts = (jnp.cumsum(doc_lengths) - doc_lengths).astype(jnp.int32)
    doc_begin = lax.optimization_barrier(jnp.max(jnp.where(starts[None, :] <= position[:, None], starts[None, :], 0), axis=1))
    return (position - doc_begin).astype(jnp.int32)

def reference(layer_queries, layer_keys, layer_values, gate_logits, norm_gain, decay_exponents, doc_lengths, out_weight):
    decay_rate = jnp.minimum(jnp.exp2(decay_exponents.astype(jnp.float32)) / TOKENS, 1.0 / 32.0)
    within = doc_positions(doc_lengths, 0, TOKENS).reshape(N_SEQ, TOK_DEV)
    query_blocks = layer_queries.reshape(N_SEQ, TOK_DEV, HEADS, HEAD_DIM)
    key_blocks = layer_keys.reshape(N_SEQ, TOK_DEV, HEADS, HEAD_DIM)
    value_blocks = layer_values.reshape(N_SEQ, TOK_DEV, HEADS, HEAD_DIM)
    gate_blocks = gate_logits.reshape(N_SEQ, TOK_DEV, HEADS * HEAD_DIM)
    local_pos = jnp.arange(TOK_DEV, dtype=jnp.int32)
    lag_grid = local_pos[:, None] - local_pos[None, :]

    def block_step(kv_state, block_data):
        query_block, key_block, value_block, gate_block, within_block = block_data
        valid_mask = (lag_grid >= 0) & (lag_grid <= within_block[:, None])
        decay_grid = jnp.where(valid_mask[None], jnp.exp(-decay_rate[:, None, None] * lag_grid[None].astype(jnp.float32)), 0.0)
        scores = jnp.einsum('thd,shd->hts', query_block.astype(jnp.float32), key_block.astype(jnp.float32))
        weights = (scores * decay_grid).astype(jnp.bfloat16)
        intra_attn = jnp.einsum('hts,shd->thd', weights.astype(jnp.float32), value_block.astype(jnp.float32))
        query_weight = jnp.where((within_block >= local_pos + 1)[:, None], jnp.exp(-decay_rate[None, :] * local_pos[:, None].astype(jnp.float32)), 0.0)
        state_rounded = kv_state.astype(jnp.bfloat16)
        cross_attn = jnp.einsum('thd,hde->the', query_block.astype(jnp.float32), state_rounded.astype(jnp.float32)) * query_weight[:, :, None]
        attention = (intra_attn + cross_attn).reshape(TOK_DEV, HEADS * HEAD_DIM)
        last_within = within_block[TOK_DEV - 1]
        carry_on = jnp.where(last_within >= TOK_DEV, jnp.exp(-decay_rate * TOK_DEV), 0.0)
        key_weight = jnp.where((local_pos >= TOK_DEV - 1 - last_within)[:, None], jnp.exp(-decay_rate[None, :] * (TOK_DEV - local_pos)[:, None].astype(jnp.float32)), 0.0)
        scaled = (key_block.astype(jnp.float32) * key_weight[:, :, None]).astype(jnp.bfloat16)
        block_state = jnp.einsum('thd,the->hde', scaled.astype(jnp.float32), value_block.astype(jnp.float32))
        new_state = carry_on[:, None, None] * kv_state + block_state
        mean_sq = lax.optimization_barrier(jnp.mean(attention * attention, axis=1))
        gated_out = (attention * lax.rsqrt(mean_sq + 1e-06)[:, None] * norm_gain.astype(jnp.float32) * jax.nn.sigmoid(gate_block.astype(jnp.float32))).astype(jnp.bfloat16)
        projected = lax.dot_general(gated_out, out_weight, (((1,), (1,)), ((), ())), preferred_element_type=jnp.float32)
        return (new_state, projected.astype(jnp.bfloat16))
    init_state = jnp.zeros((HEADS, HEAD_DIM, HEAD_DIM), jnp.float32)
    final_state, block_outs = lax.scan(block_step, init_state, (query_blocks, key_blocks, value_blocks, gate_blocks, within))
    return block_outs.reshape(TOKENS, D)
```

```python
import jax
import jax.numpy as jnp
from jax import lax
from jax.sharding import PartitionSpec as P

HEAD_DIM = 128
NT = (((1,), (1,)), ((), ()))


def begin_of(doc_lengths, position):
    count = doc_lengths.shape[0]
    order = jnp.arange(count, dtype=jnp.int32)
    ends = jnp.sum(jnp.where(order[None, :] <= order[:, None], doc_lengths[None, :], 0), axis=1)
    return jnp.sum(jnp.where(ends[None, :] <= position[:, None], doc_lengths[None, :], 0), axis=1)


def attention_parts(layer_queries, layer_keys, layer_values, decay_exponents, doc_lengths):
    tok_rows = layer_queries.shape[0]
    heads_here = decay_exponents.shape[0]
    token_span = tok_rows * lax.axis_size("seq")
    block = lax.axis_index("seq")
    decay_rate = jnp.minimum(jnp.exp2(decay_exponents.astype(jnp.float32)) / token_span, 1.0 / 32.0)
    local_pos = jnp.arange(tok_rows, dtype=jnp.int32)
    position = block * tok_rows + local_pos
    within = position - begin_of(doc_lengths, position)
    query_heads = layer_queries.reshape(tok_rows, heads_here, HEAD_DIM)
    key_heads = layer_keys.reshape(tok_rows, heads_here, HEAD_DIM)
    value_heads = layer_values.reshape(tok_rows, heads_here, HEAD_DIM)

    last_within = within[tok_rows - 1]
    key_weight = jnp.where(
        (local_pos >= tok_rows - 1 - last_within)[:, None],
        jnp.exp(-decay_rate[None, :] * (tok_rows - local_pos)[:, None].astype(jnp.float32)),
        0.0,
    )
    scaled = (key_heads.astype(jnp.float32) * key_weight[:, :, None]).astype(jnp.bfloat16)
    block_state = jnp.einsum(
        "thd,the->hde", scaled, value_heads, preferred_element_type=jnp.float32
    )

    def intra():
        lag_grid = local_pos[:, None] - local_pos[None, :]
        valid_mask = (lag_grid >= 0) & (lag_grid <= within[:, None])
        decay_grid = jnp.where(
            valid_mask[None],
            jnp.exp(-decay_rate[:, None, None] * lag_grid[None].astype(jnp.float32)),
            0.0,
        )
        scores = jnp.einsum(
            "thd,shd->hts", query_heads, key_heads, preferred_element_type=jnp.float32
        )
        weights = (scores * decay_grid).astype(jnp.bfloat16)
        return jnp.einsum("hts,shd->thd", weights, value_heads, preferred_element_type=jnp.float32)

    def cross(incoming):
        query_weight = jnp.where(
            (within >= local_pos + 1)[:, None],
            jnp.exp(-decay_rate[None, :] * local_pos[:, None].astype(jnp.float32)),
            0.0,
        )
        return (
            jnp.einsum(
                "thd,hde->the",
                query_heads,
                incoming.astype(jnp.bfloat16),
                preferred_element_type=jnp.float32,
            )
            * query_weight[:, :, None]
        )

    return decay_rate, block_state, intra, cross


def carry_of(block, decay_rate, doc_lengths, tok_rows):
    last = (block * tok_rows + tok_rows - 1)[None]
    last_within = (last - begin_of(doc_lengths, last))[0]
    return jnp.where(last_within >= tok_rows, jnp.exp(-decay_rate * tok_rows), 0.0)


def line_states(block_state, decay_rate, doc_lengths, tok_rows):
    count, block = lax.axis_size("seq"), lax.axis_index("seq")
    moving = block_state.astype(jnp.bfloat16)
    total, factor = 0.0, 1.0
    for hop in range(1, count // 2 + 1):
        moving = lax.ppermute(moving, "seq", [(i, i + 1) for i in range(hop - 1, count - 1)])
        total = total + factor * moving.astype(jnp.float32)
        carry = carry_of(block - hop, decay_rate, doc_lengths, tok_rows)
        factor = factor * carry[:, None, None]
    return total


def shards_grid(
    layer_queries,
    layer_keys,
    layer_values,
    gate_logits,
    norm_gain,
    decay_exponents,
    doc_lengths,
    out_weight,
):
    count, groups, block, head = (
        lax.axis_size("seq"),
        lax.axis_index("groups"),
        lax.axis_index("seq"),
        lax.axis_index("head"),
    )
    tok_rows = layer_queries.shape[0]
    wide = layer_queries.shape[1]
    half = out_weight.shape[0] // 2
    cut = 2 * half // 3
    cuts = ((0, cut), (cut, half))

    def hop(value, pairs):
        return lax.ppermute(value, "seq", pairs)

    def across(value, pairs):
        return lax.ppermute(
            value, ("seq", "head"), [(a * count + b, c * count + d) for a, b, c, d in pairs]
        )

    def swap(value):
        return lax.ppermute(value, "groups", [(0, 1), (1, 0)])

    mine = lax.dynamic_slice_in_dim(out_weight, groups * half, half, 0)
    parts = [mine[a:b] for a, b in cuts]
    up = [(i, i + 1) for i in range(count - 1)]
    down = [(i + 1, i) for i in range(count - 1)]

    from_low = {1: [hop(part, up) for part in parts]}
    from_high = {1: [hop(part, down) for part in parts]}
    for far in range(2, count):
        from_low[far] = [hop(part, up[far - 1 :]) for part in from_low[far - 1]]
        from_high[far] = [hop(part, down[: count - far]) for part in from_high[far - 1]]

    decay_rate, block_state, intra, cross = attention_parts(
        layer_queries, layer_keys, layer_values, decay_exponents, doc_lengths
    )
    incoming = line_states(block_state, decay_rate, doc_lengths, tok_rows)
    attention = (intra() + cross(incoming)).reshape(tok_rows, wide)
    squares = jnp.sum(attention * attention, axis=1)
    step = 1
    while step < count:
        squares = squares + lax.ppermute(squares, "head", [(i, i ^ step) for i in range(count)])
        step *= 2
    inv_scale = lax.rsqrt(squares / (wide * count) + 1e-06)
    gated = (
        attention
        * norm_gain.astype(jnp.float32)
        * jax.nn.sigmoid(gate_logits.astype(jnp.float32))
    ).astype(jnp.bfloat16)
    both = jnp.concatenate([gated, swap(gated)], axis=0)

    def product(left, weight):
        return lax.dot_general(left, weight, NT, preferred_element_type=jnp.float32)

    def collect(partial, wanted):
        total = partial
        step = 1
        while step < count:
            pairs = [
                (b, h, b, h ^ step)
                for b, f in enumerate(wanted)
                if f is not None
                for h in range(count)
                if (h ^ f) & step and not (h ^ f) & (step - 1)
            ]
            total = total + across(total.astype(jnp.bfloat16), pairs).astype(jnp.float32)
            step *= 2
        return total

    def give_back(total, wanted):
        pairs = [(g, b, f) for g in range(2) for b, f in enumerate(wanted) if f is not None]
        size = count * count
        other = lax.ppermute(
            total[tok_rows:].astype(jnp.bfloat16),
            ("groups", "seq", "head"),
            [(g * size + b * count + f, (1 - g) * size + b * count + f) for g, b, f in pairs],
        )
        return total[:tok_rows], other.astype(jnp.float32)

    result = [[], []]
    own = collect(product(gated, out_weight), list(range(count)))
    own_mask = head == block
    ends = [[], []]
    for index in range(len(cuts)):
        near = {True: 0.0, False: 0.0}
        collected = [0.0, 0.0]
        for far in range(1, count):
            lows = [b - far if b >= far else None for b in range(count)]
            highs = [b + far if b + far < count else None for b in range(count)]
            if 2 * far >= count:
                lows = [a if a is not None else b for a, b in zip(lows, highs)]
                weights = [jnp.where(block >= far, from_low[far][index], from_high[far][index])]
                tables = [lows]
            else:
                weights = [from_low[far][index], from_high[far][index]]
                tables = [lows, highs]
            for weight, table in zip(weights, tables):
                this, other = give_back(collect(product(both, weight), table), table)
                mask = head == jnp.asarray([-1 if f is None else f for f in table])[block]
                collected[0] = jnp.where(mask, this, collected[0])
                collected[1] = jnp.where(mask, other, collected[1])
        ends[0].append(collected[0])
        ends[1].append(collected[1])
    this, other = (jnp.concatenate(part, axis=1) for part in ends)
    first = groups == 0
    foreign = jnp.concatenate(
        [jnp.where(first, this, other), jnp.where(first, other, this)], axis=1
    )
    return (jnp.where(own_mask, own, foreign) * inv_scale[:, None]).astype(jnp.bfloat16)


def shards_general(
    layer_queries,
    layer_keys,
    layer_values,
    gate_logits,
    norm_gain,
    decay_exponents,
    doc_lengths,
    out_weight,
):
    tok_rows = layer_queries.shape[0]
    decay_rate, block_state, intra, cross = attention_parts(
        layer_queries, layer_keys, layer_values, decay_exponents, doc_lengths
    )
    count, block = lax.axis_size("seq"), lax.axis_index("seq")
    states = lax.all_gather(block_state, "seq")

    def turn(position, running):
        carry = carry_of(position, decay_rate, doc_lengths, tok_rows)
        longer = carry[:, None, None] * running + states[position]
        return jnp.where(position < block, longer, running)

    incoming = lax.fori_loop(0, count - 1, turn, jnp.zeros_like(block_state))
    attention = (intra() + cross(incoming)).reshape(layer_queries.shape)
    squares = lax.psum(jnp.sum(attention * attention, axis=1), "head")
    width_all = layer_queries.shape[1] * lax.axis_size("head")
    inv_scale = lax.rsqrt(squares / width_all + 1e-06)
    gated_out = (
        attention
        * inv_scale[:, None]
        * norm_gain.astype(jnp.float32)
        * jax.nn.sigmoid(gate_logits.astype(jnp.float32))
    ).astype(jnp.bfloat16)
    partials = lax.dot_general(
        gated_out,
        lax.all_gather(out_weight, "seq", axis=0, tiled=True),
        NT,
        preferred_element_type=jnp.float32,
    )
    return lax.psum_scatter(partials, "head", scatter_dimension=1, tiled=True).astype(jnp.bfloat16)


def solution(mesh):
    in_specs = (
        P(("groups", "seq"), "head"),
        P(("groups", "seq"), "head"),
        P(("groups", "seq"), "head"),
        P(("groups", "seq"), "head"),
        P("head"),
        P("head"),
        P("groups"),
        P("seq", "head"),
    )
    out_specs = P(("groups", "seq"), "head")
    seq, head = mesh.shape["seq"], mesh.shape["head"]
    grid = seq == head and seq & (seq - 1) == 0 and mesh.shape["groups"] == 2
    shards = shards_grid if grid else shards_general
    return jax.shard_map(shards, mesh=mesh, in_specs=in_specs, out_specs=out_specs, check_vma=False)
```

```python
import functools

import jax
import jax.numpy as jnp
from jax import lax
from jax.experimental import pallas as pl
from jax.experimental.pallas import tpu as pltpu
from jax.sharding import PartitionSpec as P

HEAD_DIM = 128
NT = (((1,), (1,)), ((), ()))
TN = (((0,), (0,)), ((), ()))
SMEM = pl.BlockSpec(memory_space=pltpu.SMEM)
HBM = pl.BlockSpec(memory_space=pltpu.HBM)
ANY = pl.BlockSpec(memory_space=pl.ANY)
STEPS = 4


def cost(flops, mib):
    return pl.CostEstimate(flops=int(flops), bytes_accessed=int(mib * (1 << 20)), transcendentals=0)


def begin_of(doc_lengths, position):
    count = doc_lengths.shape[0]
    order = jnp.arange(count, dtype=jnp.int32)
    ends = jnp.sum(jnp.where(order[None, :] <= order[:, None], doc_lengths[None, :], 0), axis=1)
    return jnp.sum(jnp.where(ends[None, :] <= position[:, None], doc_lengths[None, :], 0), axis=1)


def attention_parts(layer_queries, layer_keys, layer_values, decay_exponents, doc_lengths):
    tok_rows = layer_queries.shape[0]
    heads_here = decay_exponents.shape[0]
    token_span = tok_rows * lax.axis_size("seq")
    block = lax.axis_index("seq")
    decay_rate = jnp.minimum(jnp.exp2(decay_exponents.astype(jnp.float32)) / token_span, 1.0 / 32.0)
    local_pos = jnp.arange(tok_rows, dtype=jnp.int32)
    position = block * tok_rows + local_pos
    within = position - begin_of(doc_lengths, position)
    query_heads = layer_queries.reshape(tok_rows, heads_here, HEAD_DIM)
    key_heads = layer_keys.reshape(tok_rows, heads_here, HEAD_DIM)
    value_heads = layer_values.reshape(tok_rows, heads_here, HEAD_DIM)

    last_within = within[tok_rows - 1]
    key_weight = jnp.where(
        (local_pos >= tok_rows - 1 - last_within)[:, None],
        jnp.exp(-decay_rate[None, :] * (tok_rows - local_pos)[:, None].astype(jnp.float32)),
        0.0,
    )
    scaled = (key_heads.astype(jnp.float32) * key_weight[:, :, None]).astype(jnp.bfloat16)
    block_state = jnp.einsum(
        "thd,the->hde", scaled, value_heads, preferred_element_type=jnp.float32
    )

    def intra():
        lag_grid = local_pos[:, None] - local_pos[None, :]
        valid_mask = (lag_grid >= 0) & (lag_grid <= within[:, None])
        decay_grid = jnp.where(
            valid_mask[None],
            jnp.exp(-decay_rate[:, None, None] * lag_grid[None].astype(jnp.float32)),
            0.0,
        )
        scores = jnp.einsum(
            "thd,shd->hts", query_heads, key_heads, preferred_element_type=jnp.float32
        )
        weights = (scores * decay_grid).astype(jnp.bfloat16)
        return jnp.einsum("hts,shd->thd", weights, value_heads, preferred_element_type=jnp.float32)

    def cross(incoming):
        query_weight = jnp.where(
            (within >= local_pos + 1)[:, None],
            jnp.exp(-decay_rate[None, :] * local_pos[:, None].astype(jnp.float32)),
            0.0,
        )
        return (
            jnp.einsum(
                "thd,hde->the",
                query_heads,
                incoming.astype(jnp.bfloat16),
                preferred_element_type=jnp.float32,
            )
            * query_weight[:, :, None]
        )

    return decay_rate, block_state, intra, cross


def carry_of(block, decay_rate, doc_lengths, tok_rows):
    last = (block * tok_rows + tok_rows - 1)[None]
    last_within = (last - begin_of(doc_lengths, last))[0]
    return jnp.where(last_within >= tok_rows, jnp.exp(-decay_rate * tok_rows), 0.0)


def limit(mib):
    return pltpu.CompilerParams(vmem_limit_bytes=mib << 20)


def begin_at(docs, position):
    begin, end = 0, 0
    for doc in range(docs.shape[0]):
        end = end + docs[doc]
        begin = jnp.where(position >= end, end, begin)
    return begin


def row_begin(docs, block, rows):
    shape = (rows, HEAD_DIM)
    position = block * rows + lax.broadcasted_iota(jnp.int32, shape, 0)
    begin = jnp.zeros(shape, jnp.int32)
    end = 0
    for doc in range(docs.shape[0]):
        end = end + docs[doc]
        begin = jnp.where(position >= end, end, begin)
    return begin - block * rows


def rate_of(exponents, head, span):
    doubled = lax.shift_left(jnp.int32(1), exponents[head]).astype(jnp.float32)
    return jnp.minimum(doubled * (1.0 / span), 1.0 / 32.0)


def each_head(width):
    here = width // HEAD_DIM
    for n in range(here):
        yield n, pl.program_id(0) * here + n, slice(n * HEAD_DIM, (n + 1) * HEAD_DIM)


def state_kernel(where, docs, exponents, keys, values, state, *, span):
    rows, width = keys.shape
    block = where[0]
    begin = begin_at(docs, block * rows + rows - 1)
    local = lax.broadcasted_iota(jnp.int32, (rows, HEAD_DIM), 0)
    kept = local >= begin - block * rows
    left = (rows - local).astype(jnp.float32)
    for n, head, columns in each_head(width):
        weight = jnp.where(kept, jnp.exp(-rate_of(exponents, head, span) * left), 0.0)
        scaled = (keys[:, columns].astype(jnp.float32) * weight).astype(jnp.bfloat16)
        made = lax.dot_general(scaled, values[:, columns], TN, preferred_element_type=jnp.float32)
        state[n] = made.astype(jnp.bfloat16)


def intra_kernel(where, docs, exponents, queries, keys, values, out, *, span):
    rows, width = queries.shape
    part = rows // 2
    begin = row_begin(docs, where[0], rows)[:, :1]
    for step in range(2):
        low, seen = step * part, (step + 1) * part
        row = low + lax.broadcasted_iota(jnp.int32, (part, seen), 0)
        column = lax.broadcasted_iota(jnp.int32, (part, seen), 1)
        valid = (column <= row) & (column >= begin[low:seen])
        lag = (row - column).astype(jnp.float32)
        for n, head, columns in each_head(width):
            scores = lax.dot_general(
                queries[low:seen, columns], keys[:seen, columns], NT, preferred_element_type=jnp.float32
            )
            decay = jnp.exp(-rate_of(exponents, head, span) * lag)
            weights = jnp.where(valid, scores * decay, 0.0).astype(jnp.bfloat16)
            out[low:seen, columns] = jnp.dot(
                weights, values[:seen, columns], preferred_element_type=jnp.float32
            )


def gate_kernel(
    where, docs, exponents, queries, intra, near, far, gain, gate, out, squares, total, *, span
):
    rows, width = queries.shape
    block = where[0]
    local = lax.broadcasted_iota(jnp.int32, (rows, HEAD_DIM), 0).astype(jnp.float32)
    reaches = row_begin(docs, block, rows) < 0
    whole = begin_at(docs, block * rows - 1) <= (block - 1) * rows - 1

    @pl.when(pl.program_id(0) == 0)
    def _():
        total[...] = jnp.zeros_like(total)

    for n, head, columns in each_head(width):
        rate = rate_of(exponents, head, span)
        weight = jnp.where(reaches, jnp.exp(-rate * local), 0.0)
        carry = jnp.exp(jnp.full((1, HEAD_DIM), -rate * rows, jnp.float32))
        carry = jnp.where(whole, carry, 0.0)
        incoming = near[n].astype(jnp.float32) + carry * far[n].astype(jnp.float32)
        cross = jnp.dot(
            queries[:, columns], incoming.astype(jnp.bfloat16), preferred_element_type=jnp.float32
        )
        attention = intra[:, columns] + cross * weight
        opened = jax.nn.sigmoid(gate[:, columns].astype(jnp.float32))
        out[:, columns] = (attention * gain[:, columns].astype(jnp.float32) * opened).astype(
            jnp.bfloat16
        )
        total[...] += attention * attention

    @pl.when(pl.program_id(0) == pl.num_programs(0) - 1)
    def _():
        squares[...] = lax.dot_general(
            jnp.ones((8, HEAD_DIM), jnp.float32),
            total[...],
            NT,
            precision=lax.Precision.HIGHEST,
            preferred_element_type=jnp.float32,
        )


def product_kernel(*refs, lefts, weights, tile, plan):
    out, stream, sems = refs[lefts + weights :]
    copies, place = [], 0
    for n in range(weights):
        weight = refs[lefts + n]
        for start in range(0, weight.shape[0], tile):
            copies.append(
                pltpu.make_async_copy(
                    weight.at[pl.ds(start, tile)], stream.at[pl.ds(place, tile)], sems.at[place // tile]
                )
            )
            place += tile
    for copy in copies:
        copy.start()
    for first, rows, left, row, column in plan:
        left = refs[left]
        for start in range(first, first + rows, tile):
            if left is refs[0]:
                copies[start // tile].wait()
            made = lax.dot_general(
                left[...], stream[pl.ds(start, tile)], NT, preferred_element_type=jnp.float32
            )
            out[pl.ds(row, left.shape[0]), pl.ds(column + start - first, tile)] = made.astype(
                jnp.bfloat16
            )


def end_kernel(own, other, own_turned, other_turned, weight, weight_turned, *outs):
    rows = own.shape[0]
    places = outs if len(outs) == 2 else [outs[0].at[pl.ds(n * rows, rows)] for n in range(2)]
    for one, two, out in zip((own, other), (own_turned, other_turned), places):
        total = lax.dot_general(one[...], weight[...], NT, preferred_element_type=jnp.float32)
        total += lax.dot_general(
            two[...], weight_turned[...], NT, preferred_element_type=jnp.float32
        )
        out[...] = total.astype(jnp.bfloat16)


def added(one, two):
    return (one.astype(jnp.float32) + two.astype(jnp.float32)).astype(jnp.bfloat16)


def split_kernel(where, made, come, kept, sent):
    half = kept.shape[1]
    keeps_low = (where[2] ^ (where[0] - 1)) & 2 == 0
    total = added(made[...], come[...])
    for value, first, second in ((True, kept, sent), (False, sent, kept)):

        @pl.when(keeps_low == value)
        def _(first=first, second=second):
            first[...] = total[:, :half]
            second[...] = total[:, half:]


def pair_kernel(where, own, own_come, two, two_come, kept, sent):
    keeps_own = (where[2] ^ where[0]) & 2 == 0
    for value, first, second in ((True, kept, sent), (False, sent, kept)):

        @pl.when(keeps_own == value)
        def _(first=first, second=second):
            first[...] = added(own[...], own_come[...])
            second[...] = added(two[...], two_come[...])


def add_kernel(*refs):
    out, column = refs[-1], 0
    for one, two in zip(refs[:-1:2], refs[1::2]):
        here = one.shape[1]
        out[:, column : column + here] = added(one[...], two[...])
        column += here


def run(sems, *pairs):
    copies = [pltpu.make_async_copy(a, b, sems.at[n]) for n, (a, b) in enumerate(pairs)]
    for copy in copies:
        copy.start()
    for copy in copies:
        copy.wait()


def cut_kernel(where, weight, low_a, low_b, high, sems):
    rows, first = high.shape[0], low_a.shape[0]
    start = where[1] * rows

    def part(at, ref):
        return weight.at[pl.ds(pl.multiple_of(start + at, 128), ref.shape[0])], ref

    run(sems, part(0, low_a), part(0, high), part(first, low_b))


def pick_kernel(where, low, high, *refs, upper, start):
    outs, sems = refs[:-1], refs[-1]
    for above, source, offset in ((True, low, 0), (False, high, start)):

        @pl.when((where[0] >= upper) == above)
        def _(source=source, offset=offset):
            pairs, at = [], offset
            for out in outs:
                pairs.append((source.at[pl.ds(at, out.shape[0])], out))
                at += out.shape[0]
            run(sems, *pairs)


def scale_of(squares, more, width):
    mean = jnp.transpose(squares[...] + more[...])[:, :1] / width
    return lax.rsqrt(mean + 1e-06)


def at_end(where, count):
    return ((where[0] == 0) | (where[0] == count - 1)) & (where[0] ^ where[2] == count - 1)


def most_kernel(
    where, squares, squares_more, kept_a, more_a, kept_b, more_b, back, near, near_more, near_back,
    end_a, end_a_more, end_b, end_b_more, end_back, out, one, two, sems, *, width, count
):
    rows, full = out.shape
    half = full // 2
    cut = end_a.shape[1]
    scale = scale_of(squares, squares_more, width)
    apart = where[0] ^ where[2]
    end = at_end(where, count)
    beside = (apart & 1 == 1) & ~end
    low, high = pl.ds(0, rows), pl.ds(rows, rows)
    first, second = pl.ds(0, cut), pl.ds(cut, cut)
    most, others = pl.ds(0, 2 * cut), pl.ds(2 * cut, half - 2 * cut)

    def put(start, *parts):
        total = sum(part.astype(jnp.float32) for part in parts)
        out[:, pl.ds(start, parts[0].shape[1])] = (total * scale).astype(jnp.bfloat16)

    @pl.when(apart == 0)
    def _():
        run(
            sems,
            (kept_a, one.at[:, most]),
            (more_a, two.at[:, most]),
            (kept_b, one.at[:, others]),
            (more_b, two.at[:, others]),
        )
        for side in range(2):
            span = pl.ds(side * rows, rows)
            put(side * half, one[span], two[span])

    @pl.when(apart == 2)
    def _():
        run(
            sems,
            (kept_a.at[low], one.at[low, most]),
            (more_a.at[low], two.at[low, most]),
            (kept_b.at[low], one.at[low, others]),
            (more_b.at[low], two.at[low, others]),
            (back, one.at[high]),
        )

    @pl.when(beside)
    def _():
        run(
            sems,
            (near.at[low], one.at[low]),
            (near_more.at[low], two.at[low]),
            (near_back, one.at[high]),
        )

    @pl.when(end)
    def _():
        run(
            sems,
            (end_a.at[low], one.at[low, first]),
            (end_b.at[low], one.at[low, second]),
            (end_a_more.at[low], two.at[low, first]),
            (end_b_more.at[low], two.at[low, second]),
            (end_back, one.at[high, most]),
        )

    for group in range(2):
        this = group * half

        @pl.when((apart > 0) & ~end & (where[1] == group))
        def _(this=this):
            put(this, one[low], two[low])
            put(half - this, one[high])

        @pl.when(end & (where[1] == group))
        def _(this=this):
            put(this, one[low, : 2 * cut], two[low, : 2 * cut])
            put(half - this, one[high, : 2 * cut])


def last_kernel(
    where, squares, squares_more, kept, more, across, back, most, out, this, that, sems, *, width, count
):
    half, cut = out.shape[1] // 2, kept.shape[1]
    for group in range(2):

        @pl.when(at_end(where, count) & (where[1] == group))
        def _(group=group):
            scale = scale_of(squares, squares_more, width)
            for to, one, two in ((this, kept, more), (that, across, back)):
                total = one[...].astype(jnp.float32) + two[...].astype(jnp.float32)
                to[...] = (total * scale).astype(jnp.bfloat16)
            pairs = [
                (ref, out.at[:, pl.ds(side * half + half - cut, cut)])
                for ref, side in ((this, group), (that, 1 - group))
            ]
            run(sems, *pairs)


def shards_grid(
    layer_queries,
    layer_keys,
    layer_values,
    gate_logits,
    norm_gain,
    decay_exponents,
    doc_lengths,
    out_weight,
):
    count, group, block, head = (
        lax.axis_size("seq"),
        lax.axis_index("groups"),
        lax.axis_index("seq"),
        lax.axis_index("head"),
    )
    tok_rows, wide = layer_queries.shape
    heads_here = decay_exponents.shape[0]
    half = out_weight.shape[0] // 2
    cut = half // 3
    span = tok_rows * count
    index = range(count)
    table = jax.ShapeDtypeStruct

    def across(value, pairs):
        return lax.ppermute(
            value, ("seq", "head"), [(b * count + h, b * count + k) for b, h, k in pairs]
        )

    where = jnp.stack([block, group, head])

    up = [(i, i + 1) for i in range(count - 1)]
    down = [(i + 1, i) for i in range(count - 1)]
    low_a, low_b, mine = pl.pallas_call(
        cut_kernel,
        in_specs=[SMEM, HBM],
        out_shape=[
            pltpu.VMEM((rows, wide), jnp.bfloat16) for rows in (2 * cut, cut, half)
        ],
        scratch_shapes=[pltpu.SemaphoreType.DMA((3,))],
        compiler_params=limit(2),
    )(where, out_weight)
    low = [lax.ppermute(low_a, "seq", up), lax.ppermute(low_b, "seq", up)]
    high = lax.ppermute(mine, "seq", down)
    low2 = [lax.ppermute(low[n], "seq", up[1:]) for n in range(2)]
    high2 = lax.ppermute(high, "seq", down[:-1])

    def pick(part, start, outs):
        return pl.pallas_call(
            functools.partial(pick_kernel, upper=count // 2, start=start),
            in_specs=[SMEM, HBM, HBM],
            out_shape=[pltpu.VMEM((cut, wide), jnp.bfloat16)] * outs,
            scratch_shapes=[pltpu.SemaphoreType.DMA((outs,))],
            compiler_params=limit(2),
        )(where, part, high2)

    far2 = [*pick(low2[0], 0, 2), *pick(low2[1], 2 * cut, 1)]
    ends = {0: (count - 1, 1), count - 1: (0, count - 2)}
    far3 = []
    for part in far2:
        same, cross = (
            lax.ppermute(
                part,
                ("seq", "head"),
                [
                    (b * count + (h ^ turn), end * count + h)
                    for end, (f, b) in ends.items()
                    for h in index
                    if (h ^ f) & 1 == 0
                ],
            )
            for turn in (0, 1)
        )
        far3.append((same, cross))
    ends = {end: f for end, (f, _) in ends.items()}

    columns = pl.BlockSpec((tok_rows, wide // STEPS), lambda n: (0, n))
    square = pl.BlockSpec((heads_here // STEPS, HEAD_DIM, HEAD_DIM), lambda n: (n, 0, 0))
    state = pl.pallas_call(
        functools.partial(state_kernel, span=span),
        grid=(STEPS,),
        in_specs=[SMEM, SMEM, SMEM, columns, columns],
        out_specs=square,
        out_shape=table((heads_here, HEAD_DIM, HEAD_DIM), jnp.bfloat16),
        compiler_params=limit(8),
    )(where, doc_lengths, decay_exponents, layer_keys, layer_values)
    near_state = lax.ppermute(state, "seq", up)
    far_state = lax.ppermute(state, "seq", [(i, i + 2) for i in range(count - 2)])
    intra = pl.pallas_call(
        functools.partial(intra_kernel, span=span),
        grid=(STEPS,),
        in_specs=[SMEM, SMEM, SMEM, columns, columns, columns],
        out_specs=columns,
        out_shape=table((tok_rows, wide), jnp.float32),
        compiler_params=limit(12),
    )(where, doc_lengths, decay_exponents, layer_queries, layer_keys, layer_values)
    gated, squares = pl.pallas_call(
        functools.partial(gate_kernel, span=span),
        grid=(STEPS,),
        in_specs=[
            SMEM, SMEM, SMEM, columns, columns, square, square,
            pl.BlockSpec((1, wide // STEPS), lambda n: (0, n)), columns,
        ],
        out_specs=[columns, pl.BlockSpec((8, tok_rows), lambda n: (0, 0))],
        out_shape=[table((tok_rows, wide), jnp.bfloat16), table((8, tok_rows), jnp.float32)],
        scratch_shapes=[pltpu.VMEM((tok_rows, HEAD_DIM), jnp.float32)],
        compiler_params=limit(12),
    )(
        where, doc_lengths, decay_exponents, layer_queries, intra, near_state, far_state,
        norm_gain[None, :], gate_logits,
    )
    other = lax.ppermute(gated, "groups", [(0, 1), (1, 0)])
    turned = [
        across(value, [(b, h, h ^ 1) for b in index for h in index])
        for value in (gated, other)
    ]
    squares = squares + lax.ppermute(squares, "head", [(i, i ^ 1) for i in index])
    squares_more = lax.ppermute(squares, "head", [(i, i ^ 2) for i in index])

    def product(shape, lefts, weights, plan, space=ANY):
        total = sum(weight.shape[0] for weight in weights)
        tile = 256
        return pl.pallas_call(
            functools.partial(
                product_kernel, lefts=len(lefts), weights=len(weights), tile=tile, plan=plan
            ),
            in_specs=[pl.BlockSpec()] * len(lefts) + [space] * len(weights),
            out_shape=pltpu.VMEM(shape, jnp.bfloat16),
            scratch_shapes=[
                pltpu.VMEM((total, wide), jnp.bfloat16),
                pltpu.SemaphoreType.DMA((total // tile,)),
            ],
            compiler_params=limit(12),
            cost_estimate=cost(2 * shape[0] * shape[1] * wide, 8),
        )(*lefts, *weights)

    def for_both(*weights):
        plan, column = [], 0
        for weight in weights:
            rows = weight.shape[0]
            plan += [(column, rows, side, side * tok_rows, column) for side in range(2)]
            column += rows
        return product((2 * tok_rows, column), (gated, other), weights, plan)

    def split(made, come):
        rows = 2 * tok_rows // STEPS
        return pl.pallas_call(
            split_kernel,
            grid=(STEPS,),
            in_specs=[SMEM] + [pl.BlockSpec((rows, 2 * half), lambda n: (n, 0))] * 2,
            out_specs=[pl.BlockSpec((rows, half), lambda n: (n, 0))] * 2,
            out_shape=[pltpu.VMEM((2 * tok_rows, half), jnp.bfloat16)] * 2,
            compiler_params=limit(8),
            cost_estimate=cost(4 * tok_rows * half, 9),
        )(where, made, come)

    def pair(own, two, start):
        rows, width = two[0].shape
        size = (rows // 2, cut)
        shifted = pl.BlockSpec(size, lambda n, c: (n, c + start // cut))
        plain = pl.BlockSpec(size, lambda n, c: (n, c))
        return pl.pallas_call(
            pair_kernel,
            grid=(2, width // cut),
            in_specs=[SMEM, shifted, shifted, plain, plain],
            out_specs=[plain, plain],
            out_shape=[pltpu.VMEM((rows, width), jnp.bfloat16)] * 2,
            compiler_params=limit(8),
            cost_estimate=cost(rows * width, 6),
        )(where, *own, *two)

    def add(*pairs, part=0, parts=1):
        rows, width = pairs[0][0].shape[0] // parts, sum(one.shape[1] for one, _ in pairs)
        steps = 2
        operands = [value for pair in pairs for value in pair]

        def block(width, part=0):
            return pl.BlockSpec((rows // steps, width), lambda n: (part * steps + n, 0))

        return pl.pallas_call(
            add_kernel,
            grid=(steps,),
            in_specs=[block(value.shape[1], part) for value in operands],
            out_specs=block(width),
            out_shape=pltpu.VMEM((rows, width), jnp.bfloat16),
            compiler_params=limit(6),
            cost_estimate=cost(rows * width, 3),
        )(*operands)

    def from_core(made, wanted):
        pairs = [(b, h, h ^ 1) for b, f in wanted.items() for h in index if (h ^ f) & 1]
        return across(made, pairs)

    def anywhere(value, pairs):
        flat = [tuple((g * count + b) * count + h for g, b, h in pair) for pair in pairs]
        return lax.ppermute(value, ("groups", "seq", "head"), flat)

    def give_back(total, owners):
        return anywhere(total, [((g, b, f), (1 - g, b, f)) for g in range(2) for b, f in owners])

    plan = [(side * half, half, 0, side * tok_rows, 0) for side in range(2)]
    made = product((2 * tok_rows, half), (gated,), (out_weight,), plan, HBM)
    own = (made, from_core(made, {b: b for b in index}))

    nears = [(b, f) for b in index for f in (b - 1, b + 1) if 0 <= f < count]
    made = for_both(*low, high)
    come = from_core(made, {b: f for b, f in nears})
    near_kept, near_sent = split(made, come)
    near_more = across(near_sent, [(b, f ^ 2, f) for b, f in nears])
    near_back = give_back(add((near_kept, near_more), part=1, parts=2), nears)

    pieces = []
    for n, part in enumerate((far2[:2], far2[2:])):
        made = for_both(*part)
        two = (made, from_core(made, {b: b ^ 2 for b in index}))
        kept, sent = pair(own, two, 2 * n * cut)
        more = across(sent, [(b, h, h ^ 2) for b in index for h in (b, b ^ 2)])
        pieces.append((kept, more))
    back = give_back(add(*pieces, part=1, parts=2), [(b, b ^ 2) for b in index])

    last = []
    for n, part in enumerate(far3):
        parts = 1 if n < 2 else 2
        made = pl.pallas_call(
            end_kernel,
            out_shape=[pltpu.VMEM((2 * tok_rows // parts, cut), jnp.bfloat16)] * parts,
            compiler_params=limit(12),
            cost_estimate=cost(8 * tok_rows * cut * wide, 8),
        )(gated, other, *turned, *part)
        last.append((made[0], across(made[0], [(b, f ^ 2, f) for b, f in ends.items()])))
    first_back = give_back(add(*last[:2], part=1, parts=2), ends.items())
    pairs = [((g, b, f ^ 2), (1 - g, b, f)) for g in range(2) for b, f in ends.items()]
    last_back = anywhere(made[1], pairs), give_back(made[1], ends.items())

    sizes = {"width": wide * count, "count": count}
    most = pl.pallas_call(
        functools.partial(most_kernel, **sizes),
        in_specs=[SMEM, pl.BlockSpec(), pl.BlockSpec()] + [ANY] * 13,
        out_shape=table((tok_rows, 2 * half), jnp.bfloat16),
        scratch_shapes=[
            pltpu.VMEM((2 * tok_rows, half), jnp.bfloat16),
            pltpu.VMEM((2 * tok_rows, half), jnp.bfloat16),
            pltpu.SemaphoreType.DMA((6,)),
        ],
        compiler_params=limit(8),
    )(
        where, squares, squares_more, *pieces[0], *pieces[1], back,
        near_kept, near_more, near_back, *last[0], *last[1], first_back,
    )
    return pl.pallas_call(
        functools.partial(last_kernel, **sizes),
        in_specs=[SMEM] + [pl.BlockSpec()] * 6 + [HBM],
        out_specs=HBM,
        out_shape=table((tok_rows, 2 * half), jnp.bfloat16),
        scratch_shapes=[
            pltpu.VMEM((tok_rows, cut), jnp.bfloat16),
            pltpu.VMEM((tok_rows, cut), jnp.bfloat16),
            pltpu.SemaphoreType.DMA((2,)),
        ],
        input_output_aliases={7: 0},
        compiler_params=limit(4),
    )(where, squares, squares_more, *last[2], *last_back, most)


def shards_general(
    layer_queries,
    layer_keys,
    layer_values,
    gate_logits,
    norm_gain,
    decay_exponents,
    doc_lengths,
    out_weight,
):
    tok_rows = layer_queries.shape[0]
    decay_rate, block_state, intra, cross = attention_parts(
        layer_queries, layer_keys, layer_values, decay_exponents, doc_lengths
    )
    count, block = lax.axis_size("seq"), lax.axis_index("seq")
    states = lax.all_gather(block_state, "seq")

    def turn(position, running):
        carry = carry_of(position, decay_rate, doc_lengths, tok_rows)
        longer = carry[:, None, None] * running + states[position]
        return jnp.where(position < block, longer, running)

    incoming = lax.fori_loop(0, count - 1, turn, jnp.zeros_like(block_state))
    attention = (intra() + cross(incoming)).reshape(layer_queries.shape)
    squares = lax.psum(jnp.sum(attention * attention, axis=1), "head")
    width_all = layer_queries.shape[1] * lax.axis_size("head")
    inv_scale = lax.rsqrt(squares / width_all + 1e-06)
    gated_out = (
        attention
        * inv_scale[:, None]
        * norm_gain.astype(jnp.float32)
        * jax.nn.sigmoid(gate_logits.astype(jnp.float32))
    ).astype(jnp.bfloat16)
    partials = lax.dot_general(
        gated_out,
        lax.all_gather(out_weight, "seq", axis=0, tiled=True),
        NT,
        preferred_element_type=jnp.float32,
    )
    return lax.psum_scatter(partials, "head", scatter_dimension=1, tiled=True).astype(jnp.bfloat16)


def solution(mesh):
    in_specs = (
        P(("groups", "seq"), "head"),
        P(("groups", "seq"), "head"),
        P(("groups", "seq"), "head"),
        P(("groups", "seq"), "head"),
        P("head"),
        P("head"),
        P("groups"),
        P("seq", "head"),
    )
    out_specs = P(("groups", "seq"), "head")
    seq, head = mesh.shape["seq"], mesh.shape["head"]
    grid = seq == head == 4 and mesh.shape["groups"] == 2
    shards = shards_grid if grid else shards_general
    return jax.shard_map(shards, mesh=mesh, in_specs=in_specs, out_specs=out_specs, check_vma=False)
```

```python
import functools

import jax
import jax.numpy as jnp
from jax import lax
from jax.experimental import pallas as pl
from jax.experimental.pallas import tpu as pltpu
from jax.sharding import PartitionSpec as P

HEAD_DIM = 128
NT = (((1,), (1,)), ((), ()))
TN = (((0,), (0,)), ((), ()))
SMEM = pl.BlockSpec(memory_space=pltpu.SMEM)
HBM = pl.BlockSpec(memory_space=pltpu.HBM)
ANY = pl.BlockSpec(memory_space=pl.ANY)
STEPS = 4


def cost(flops, mib):
    return pl.CostEstimate(flops=int(flops), bytes_accessed=int(mib * (1 << 20)), transcendentals=0)


def begin_of(doc_lengths, position):
    count = doc_lengths.shape[0]
    order = jnp.arange(count, dtype=jnp.int32)
    ends = jnp.sum(jnp.where(order[None, :] <= order[:, None], doc_lengths[None, :], 0), axis=1)
    return jnp.sum(jnp.where(ends[None, :] <= position[:, None], doc_lengths[None, :], 0), axis=1)


def attention_parts(layer_queries, layer_keys, layer_values, decay_exponents, doc_lengths):
    tok_rows = layer_queries.shape[0]
    heads_here = decay_exponents.shape[0]
    token_span = tok_rows * lax.axis_size("seq")
    block = lax.axis_index("seq")
    decay_rate = jnp.minimum(jnp.exp2(decay_exponents.astype(jnp.float32)) / token_span, 1.0 / 32.0)
    local_pos = jnp.arange(tok_rows, dtype=jnp.int32)
    position = block * tok_rows + local_pos
    within = position - begin_of(doc_lengths, position)
    query_heads = layer_queries.reshape(tok_rows, heads_here, HEAD_DIM)
    key_heads = layer_keys.reshape(tok_rows, heads_here, HEAD_DIM)
    value_heads = layer_values.reshape(tok_rows, heads_here, HEAD_DIM)

    last_within = within[tok_rows - 1]
    key_weight = jnp.where(
        (local_pos >= tok_rows - 1 - last_within)[:, None],
        jnp.exp(-decay_rate[None, :] * (tok_rows - local_pos)[:, None].astype(jnp.float32)),
        0.0,
    )
    scaled = (key_heads.astype(jnp.float32) * key_weight[:, :, None]).astype(jnp.bfloat16)
    block_state = jnp.einsum(
        "thd,the->hde", scaled, value_heads, preferred_element_type=jnp.float32
    )

    def intra():
        lag_grid = local_pos[:, None] - local_pos[None, :]
        valid_mask = (lag_grid >= 0) & (lag_grid <= within[:, None])
        decay_grid = jnp.where(
            valid_mask[None],
            jnp.exp(-decay_rate[:, None, None] * lag_grid[None].astype(jnp.float32)),
            0.0,
        )
        scores = jnp.einsum(
            "thd,shd->hts", query_heads, key_heads, preferred_element_type=jnp.float32
        )
        weights = (scores * decay_grid).astype(jnp.bfloat16)
        return jnp.einsum("hts,shd->thd", weights, value_heads, preferred_element_type=jnp.float32)

    def cross(incoming):
        query_weight = jnp.where(
            (within >= local_pos + 1)[:, None],
            jnp.exp(-decay_rate[None, :] * local_pos[:, None].astype(jnp.float32)),
            0.0,
        )
        return (
            jnp.einsum(
                "thd,hde->the",
                query_heads,
                incoming.astype(jnp.bfloat16),
                preferred_element_type=jnp.float32,
            )
            * query_weight[:, :, None]
        )

    return decay_rate, block_state, intra, cross


def carry_of(block, decay_rate, doc_lengths, tok_rows):
    last = (block * tok_rows + tok_rows - 1)[None]
    last_within = (last - begin_of(doc_lengths, last))[0]
    return jnp.where(last_within >= tok_rows, jnp.exp(-decay_rate * tok_rows), 0.0)


def limit(mib):
    return pltpu.CompilerParams(vmem_limit_bytes=mib << 20)


def begin_at(docs, position):
    begin, end = 0, 0
    for doc in range(docs.shape[0]):
        end = end + docs[doc]
        begin = jnp.where(position >= end, end, begin)
    return begin


def row_begin(docs, block, rows):
    shape = (rows, HEAD_DIM)
    position = block * rows + lax.broadcasted_iota(jnp.int32, shape, 0)
    begin = jnp.zeros(shape, jnp.int32)
    end = 0
    for doc in range(docs.shape[0]):
        end = end + docs[doc]
        begin = jnp.where(position >= end, end, begin)
    return begin - block * rows


def rate_of(exponents, head, span):
    doubled = lax.shift_left(jnp.int32(1), exponents[head]).astype(jnp.float32)
    return jnp.minimum(doubled * (1.0 / span), 1.0 / 32.0)


def each_head(width):
    here = width // HEAD_DIM
    for n in range(here):
        yield n, pl.program_id(0) * here + n, slice(n * HEAD_DIM, (n + 1) * HEAD_DIM)


def state_kernel(where, docs, exponents, keys, values, state, *, span):
    rows, width = keys.shape
    block = where[0]
    begin = begin_at(docs, block * rows + rows - 1)
    local = lax.broadcasted_iota(jnp.int32, (rows, HEAD_DIM), 0)
    kept = local >= begin - block * rows
    left = (rows - local).astype(jnp.float32)
    for n, head, columns in each_head(width):
        weight = jnp.where(kept, jnp.exp(-rate_of(exponents, head, span) * left), 0.0)
        scaled = (keys[:, columns].astype(jnp.float32) * weight).astype(jnp.bfloat16)
        made = lax.dot_general(scaled, values[:, columns], TN, preferred_element_type=jnp.float32)
        state[n] = made.astype(jnp.bfloat16)


def intra_kernel(where, docs, exponents, queries, keys, values, out, *, span):
    rows, width = queries.shape
    part = rows // 2
    begin = row_begin(docs, where[0], rows)[:, :1]
    for step in range(2):
        low, seen = step * part, (step + 1) * part
        row = low + lax.broadcasted_iota(jnp.int32, (part, seen), 0)
        column = lax.broadcasted_iota(jnp.int32, (part, seen), 1)
        valid = (column <= row) & (column >= begin[low:seen])
        lag = (row - column).astype(jnp.float32)
        for n, head, columns in each_head(width):
            scores = lax.dot_general(
                queries[low:seen, columns], keys[:seen, columns], NT, preferred_element_type=jnp.float32
            )
            decay = jnp.exp(-rate_of(exponents, head, span) * lag)
            weights = jnp.where(valid, scores * decay, 0.0).astype(jnp.bfloat16)
            out[low:seen, columns] = jnp.dot(
                weights, values[:seen, columns], preferred_element_type=jnp.float32
            )


def gate_kernel(
    where, docs, exponents, queries, intra, near, far, gain, gate, out, squares, total, *, span
):
    rows, width = queries.shape
    block = where[0]
    local = lax.broadcasted_iota(jnp.int32, (rows, HEAD_DIM), 0).astype(jnp.float32)
    reaches = row_begin(docs, block, rows) < 0
    whole = begin_at(docs, block * rows - 1) <= (block - 1) * rows - 1

    @pl.when(pl.program_id(0) == 0)
    def _():
        total[...] = jnp.zeros_like(total)

    for n, head, columns in each_head(width):
        rate = rate_of(exponents, head, span)
        weight = jnp.where(reaches, jnp.exp(-rate * local), 0.0)
        carry = jnp.exp(jnp.full((1, HEAD_DIM), -rate * rows, jnp.float32))
        carry = jnp.where(whole, carry, 0.0)
        incoming = near[n].astype(jnp.float32) + carry * far[n].astype(jnp.float32)
        cross = jnp.dot(
            queries[:, columns], incoming.astype(jnp.bfloat16), preferred_element_type=jnp.float32
        )
        attention = intra[:, columns] + cross * weight
        opened = jax.nn.sigmoid(gate[:, columns].astype(jnp.float32))
        out[:, columns] = (attention * gain[:, columns].astype(jnp.float32) * opened).astype(
            jnp.bfloat16
        )
        total[...] += attention * attention

    @pl.when(pl.program_id(0) == pl.num_programs(0) - 1)
    def _():
        squares[...] = lax.dot_general(
            jnp.ones((8, HEAD_DIM), jnp.float32),
            total[...],
            NT,
            precision=lax.Precision.HIGHEST,
            preferred_element_type=jnp.float32,
        )


def product_kernel(*refs, lefts, weights, tile, plan):
    out, stream, sems = refs[lefts + weights :]
    copies, place = [], 0
    for n in range(weights):
        weight = refs[lefts + n]
        for start in range(0, weight.shape[0], tile):
            copies.append(
                pltpu.make_async_copy(
                    weight.at[pl.ds(start, tile)], stream.at[pl.ds(place, tile)], sems.at[place // tile]
                )
            )
            place += tile
    for copy in copies:
        copy.start()
    for first, rows, left, row, column in plan:
        left = refs[left]
        for start in range(first, first + rows, tile):
            if left is refs[0]:
                copies[start // tile].wait()
            made = lax.dot_general(
                left[...], stream[pl.ds(start, tile)], NT, preferred_element_type=jnp.float32
            )
            out[pl.ds(row, left.shape[0]), pl.ds(column + start - first, tile)] = made.astype(
                jnp.bfloat16
            )


def end_kernel(own, other, own_turned, other_turned, weight, weight_turned, *outs):
    rows = own.shape[0]
    places = outs if len(outs) == 2 else [outs[0].at[pl.ds(n * rows, rows)] for n in range(2)]
    for one, two, out in zip((own, other), (own_turned, other_turned), places):
        total = lax.dot_general(one[...], weight[...], NT, preferred_element_type=jnp.float32)
        total += lax.dot_general(
            two[...], weight_turned[...], NT, preferred_element_type=jnp.float32
        )
        out[...] = total.astype(jnp.bfloat16)


def added(one, two):
    return (one.astype(jnp.float32) + two.astype(jnp.float32)).astype(jnp.bfloat16)


def split_kernel(where, made, come, kept, sent):
    half = kept.shape[1]
    keeps_low = (where[2] ^ (where[0] - 1)) & 2 == 0
    total = added(made[...], come[...])
    for value, first, second in ((True, kept, sent), (False, sent, kept)):

        @pl.when(keeps_low == value)
        def _(first=first, second=second):
            first[...] = total[:, :half]
            second[...] = total[:, half:]


def pair_kernel(where, own, own_come, two, two_come, kept, sent):
    keeps_own = (where[2] ^ where[0]) & 2 == 0
    for value, first, second in ((True, kept, sent), (False, sent, kept)):

        @pl.when(keeps_own == value)
        def _(first=first, second=second):
            first[...] = added(own[...], own_come[...])
            second[...] = added(two[...], two_come[...])


def add_kernel(*refs):
    out, column = refs[-1], 0
    for one, two in zip(refs[:-1:2], refs[1::2]):
        here = one.shape[1]
        out[:, column : column + here] = added(one[...], two[...])
        column += here


def run(sems, *pairs):
    copies = [pltpu.make_async_copy(a, b, sems.at[n]) for n, (a, b) in enumerate(pairs)]
    for copy in copies:
        copy.start()
    for copy in copies:
        copy.wait()


def cut_kernel(where, weight, low_a, low_b, high, sems):
    rows, first = high.shape[0], low_a.shape[0]
    start = where[1] * rows

    def part(at, ref):
        return weight.at[pl.ds(pl.multiple_of(start + at, 128), ref.shape[0])], ref

    run(sems, part(0, low_a), part(0, high), part(first, low_b))


def pick_kernel(where, low, high, *refs, upper, start):
    outs, sems = refs[:-1], refs[-1]
    for above, source, offset in ((True, low, 0), (False, high, start)):

        @pl.when((where[0] >= upper) == above)
        def _(source=source, offset=offset):
            pairs, at = [], offset
            for out in outs:
                pairs.append((source.at[pl.ds(at, out.shape[0])], out))
                at += out.shape[0]
            run(sems, *pairs)


def scale_of(squares, more, width):
    mean = jnp.transpose(squares[...] + more[...])[:, :1] / width
    return lax.rsqrt(mean + 1e-06)


def at_end(where, count):
    return ((where[0] == 0) | (where[0] == count - 1)) & (where[0] ^ where[2] == count - 1)


def most_kernel(
    where, squares, squares_more, kept_a, more_a, back_a, kept_b, more_b, back_b, near, near_more, near_back,
    end_a, end_a_more, end_a_back, end_b, end_b_more, end_b_across, end_b_back, out, one, two, sems,
    *, width, count
):
    rows, full = out.shape
    half = full // 2
    cut = end_a.shape[1]
    scale = scale_of(squares, squares_more, width)
    apart = where[0] ^ where[2]
    end = at_end(where, count)
    beside = (apart & 1 == 1) & ~end
    low, high = pl.ds(0, rows), pl.ds(rows, rows)
    first, second = pl.ds(0, cut), pl.ds(cut, cut)
    most, others = pl.ds(0, 2 * cut), pl.ds(2 * cut, half - 2 * cut)

    def put(start, *parts):
        total = sum(part.astype(jnp.float32) for part in parts)
        out[:, pl.ds(start, parts[0].shape[1])] = (total * scale).astype(jnp.bfloat16)

    @pl.when(apart == 0)
    def _():
        run(
            sems,
            (kept_a, one.at[:, most]),
            (more_a, two.at[:, most]),
            (kept_b, one.at[:, others]),
            (more_b, two.at[:, others]),
        )
        for side in range(2):
            span = pl.ds(side * rows, rows)
            put(side * half, one[span], two[span])

    @pl.when(apart == 2)
    def _():
        run(
            sems,
            (kept_a.at[low], one.at[low, most]),
            (more_a.at[low], two.at[low, most]),
            (kept_b.at[low], one.at[low, others]),
            (more_b.at[low], two.at[low, others]),
            (back_a, one.at[high, most]),
            (back_b, one.at[high, others]),
        )

    @pl.when(beside)
    def _():
        run(
            sems,
            (near.at[low], one.at[low]),
            (near_more.at[low], two.at[low]),
            (near_back, one.at[high]),
        )

    @pl.when(end)
    def _():
        run(
            sems,
            (end_a.at[low], one.at[low, first]),
            (end_b.at[low], one.at[low, second]),
            (end_a_more.at[low], two.at[low, first]),
            (end_b_more.at[low], two.at[low, second]),
            (end_a_back, one.at[high, first]),
            (end_b_across, one.at[high, second]),
            (end_b_back, two.at[high, second]),
        )

    for group in range(2):
        this = group * half

        @pl.when((apart > 0) & ~end & (where[1] == group))
        def _(this=this):
            put(this, one[low], two[low])
            put(half - this, one[high])

        @pl.when(end & (where[1] == group))
        def _(this=this):
            put(this, one[low, : 2 * cut], two[low, : 2 * cut])
            put(half - this, one[high, :cut])
            put(half - this + cut, one[high, cut : 2 * cut], two[high, cut : 2 * cut])


def last_kernel(
    where, squares, squares_more, kept, more, across, back, most, out, this, that, sems, *, width, count
):
    half, cut = out.shape[1] // 2, kept.shape[1]
    for group in range(2):

        @pl.when(at_end(where, count) & (where[1] == group))
        def _(group=group):
            scale = scale_of(squares, squares_more, width)
            for to, one, two in ((this, kept, more), (that, across, back)):
                total = one[...].astype(jnp.float32) + two[...].astype(jnp.float32)
                to[...] = (total * scale).astype(jnp.bfloat16)
            pairs = [
                (ref, out.at[:, pl.ds(side * half + half - cut, cut)])
                for ref, side in ((this, group), (that, 1 - group))
            ]
            run(sems, *pairs)


def shards_grid(
    layer_queries,
    layer_keys,
    layer_values,
    gate_logits,
    norm_gain,
    decay_exponents,
    doc_lengths,
    out_weight,
):
    count, group, block, head = (
        lax.axis_size("seq"),
        lax.axis_index("groups"),
        lax.axis_index("seq"),
        lax.axis_index("head"),
    )
    tok_rows, wide = layer_queries.shape
    heads_here = decay_exponents.shape[0]
    half = out_weight.shape[0] // 2
    cut = half // 3
    span = tok_rows * count
    index = range(count)
    table = jax.ShapeDtypeStruct

    def across(value, pairs):
        return lax.ppermute(
            value, ("seq", "head"), [(b * count + h, b * count + k) for b, h, k in pairs]
        )

    where = jnp.stack([block, group, head])

    up = [(i, i + 1) for i in range(count - 1)]
    down = [(i + 1, i) for i in range(count - 1)]
    low_a, low_b, mine = pl.pallas_call(
        cut_kernel,
        in_specs=[SMEM, HBM],
        out_shape=[
            pltpu.VMEM((rows, wide), jnp.bfloat16) for rows in (2 * cut, cut, half)
        ],
        scratch_shapes=[pltpu.SemaphoreType.DMA((3,))],
        compiler_params=limit(2),
    )(where, out_weight)
    low = [lax.ppermute(low_a, "seq", up), lax.ppermute(low_b, "seq", up)]
    high = lax.ppermute(mine, "seq", down)
    low2 = [lax.ppermute(low[n], "seq", up[1:]) for n in range(2)]
    high2 = lax.ppermute(high, "seq", down[:-1])

    def pick(part, start, outs):
        return pl.pallas_call(
            functools.partial(pick_kernel, upper=count // 2, start=start),
            in_specs=[SMEM, HBM, HBM],
            out_shape=[pltpu.VMEM((cut, wide), jnp.bfloat16)] * outs,
            scratch_shapes=[pltpu.SemaphoreType.DMA((outs,))],
            compiler_params=limit(2),
        )(where, part, high2)

    far2 = [*pick(low2[0], 0, 2), *pick(low2[1], 2 * cut, 1)]
    ends = {0: (count - 1, 1), count - 1: (0, count - 2)}
    far3 = []
    for part in far2:
        same, cross = (
            lax.ppermute(
                part,
                ("seq", "head"),
                [
                    (b * count + (h ^ turn), end * count + h)
                    for end, (f, b) in ends.items()
                    for h in index
                    if (h ^ f) & 1 == 0
                ],
            )
            for turn in (0, 1)
        )
        far3.append((same, cross))
    ends = {end: f for end, (f, _) in ends.items()}

    columns = pl.BlockSpec((tok_rows, wide // STEPS), lambda n: (0, n))
    square = pl.BlockSpec((heads_here // STEPS, HEAD_DIM, HEAD_DIM), lambda n: (n, 0, 0))
    state = pl.pallas_call(
        functools.partial(state_kernel, span=span),
        grid=(STEPS,),
        in_specs=[SMEM, SMEM, SMEM, columns, columns],
        out_specs=square,
        out_shape=table((heads_here, HEAD_DIM, HEAD_DIM), jnp.bfloat16),
        compiler_params=limit(8),
    )(where, doc_lengths, decay_exponents, layer_keys, layer_values)
    near_state = lax.ppermute(state, "seq", up)
    far_state = lax.ppermute(state, "seq", [(i, i + 2) for i in range(count - 2)])
    intra = pl.pallas_call(
        functools.partial(intra_kernel, span=span),
        grid=(STEPS,),
        in_specs=[SMEM, SMEM, SMEM, columns, columns, columns],
        out_specs=columns,
        out_shape=table((tok_rows, wide), jnp.float32),
        compiler_params=limit(12),
    )(where, doc_lengths, decay_exponents, layer_queries, layer_keys, layer_values)
    gated, squares = pl.pallas_call(
        functools.partial(gate_kernel, span=span),
        grid=(STEPS,),
        in_specs=[
            SMEM, SMEM, SMEM, columns, columns, square, square,
            pl.BlockSpec((1, wide // STEPS), lambda n: (0, n)), columns,
        ],
        out_specs=[columns, pl.BlockSpec((8, tok_rows), lambda n: (0, 0))],
        out_shape=[table((tok_rows, wide), jnp.bfloat16), table((8, tok_rows), jnp.float32)],
        scratch_shapes=[pltpu.VMEM((tok_rows, HEAD_DIM), jnp.float32)],
        compiler_params=limit(12),
    )(
        where, doc_lengths, decay_exponents, layer_queries, intra, near_state, far_state,
        norm_gain[None, :], gate_logits,
    )
    other = lax.ppermute(gated, "groups", [(0, 1), (1, 0)])
    turned = [
        across(value, [(b, h, h ^ 1) for b in index for h in index])
        for value in (gated, other)
    ]
    squares = squares + lax.ppermute(squares, "head", [(i, i ^ 1) for i in index])
    squares_more = lax.ppermute(squares, "head", [(i, i ^ 2) for i in index])

    def product(shape, lefts, weights, plan, space=ANY):
        total = sum(weight.shape[0] for weight in weights)
        tile = 256
        return pl.pallas_call(
            functools.partial(
                product_kernel, lefts=len(lefts), weights=len(weights), tile=tile, plan=plan
            ),
            in_specs=[pl.BlockSpec()] * len(lefts) + [space] * len(weights),
            out_shape=pltpu.VMEM(shape, jnp.bfloat16),
            scratch_shapes=[
                pltpu.VMEM((total, wide), jnp.bfloat16),
                pltpu.SemaphoreType.DMA((total // tile,)),
            ],
            compiler_params=limit(12),
            cost_estimate=cost(2 * shape[0] * shape[1] * wide, 8),
        )(*lefts, *weights)

    def for_both(*weights):
        plan, column = [], 0
        for weight in weights:
            rows = weight.shape[0]
            plan += [(column, rows, side, side * tok_rows, column) for side in range(2)]
            column += rows
        return product((2 * tok_rows, column), (gated, other), weights, plan)

    def split(made, come):
        rows = 2 * tok_rows // STEPS
        return pl.pallas_call(
            split_kernel,
            grid=(STEPS,),
            in_specs=[SMEM] + [pl.BlockSpec((rows, 2 * half), lambda n: (n, 0))] * 2,
            out_specs=[pl.BlockSpec((rows, half), lambda n: (n, 0))] * 2,
            out_shape=[pltpu.VMEM((2 * tok_rows, half), jnp.bfloat16)] * 2,
            compiler_params=limit(8),
            cost_estimate=cost(4 * tok_rows * half, 9),
        )(where, made, come)

    def pair(own, two, start):
        rows, width = two[0].shape
        size = (rows // 2, cut)
        shifted = pl.BlockSpec(size, lambda n, c: (n, c + start // cut))
        plain = pl.BlockSpec(size, lambda n, c: (n, c))
        return pl.pallas_call(
            pair_kernel,
            grid=(2, width // cut),
            in_specs=[SMEM, shifted, shifted, plain, plain],
            out_specs=[plain, plain],
            out_shape=[pltpu.VMEM((rows, width), jnp.bfloat16)] * 2,
            compiler_params=limit(8),
            cost_estimate=cost(rows * width, 6),
        )(where, *own, *two)

    def add(*pairs, part=0, parts=1):
        rows, width = pairs[0][0].shape[0] // parts, sum(one.shape[1] for one, _ in pairs)
        steps = 2
        operands = [value for pair in pairs for value in pair]

        def block(width, part=0):
            return pl.BlockSpec((rows // steps, width), lambda n: (part * steps + n, 0))

        return pl.pallas_call(
            add_kernel,
            grid=(steps,),
            in_specs=[block(value.shape[1], part) for value in operands],
            out_specs=block(width),
            out_shape=pltpu.VMEM((rows, width), jnp.bfloat16),
            compiler_params=limit(6),
            cost_estimate=cost(rows * width, 3),
        )(*operands)

    def from_core(made, wanted):
        pairs = [(b, h, h ^ 1) for b, f in wanted.items() for h in index if (h ^ f) & 1]
        return across(made, pairs)

    def anywhere(value, pairs):
        flat = [tuple((g * count + b) * count + h for g, b, h in pair) for pair in pairs]
        return lax.ppermute(value, ("groups", "seq", "head"), flat)

    def give_back(total, owners):
        return anywhere(total, [((g, b, f), (1 - g, b, f)) for g in range(2) for b, f in owners])

    plan = [(side * half, half, 0, side * tok_rows, 0) for side in range(2)]
    made = product((2 * tok_rows, half), (gated,), (out_weight,), plan, HBM)
    own = (made, from_core(made, {b: b for b in index}))

    nears = [(b, f) for b in index for f in (b - 1, b + 1) if 0 <= f < count]
    made = for_both(*low, high)
    come = from_core(made, {b: f for b, f in nears})
    near_kept, near_sent = split(made, come)
    near_more = across(near_sent, [(b, f ^ 2, f) for b, f in nears])
    near_back = give_back(add((near_kept, near_more), part=1, parts=2), nears)

    pieces = []
    for n, part in enumerate((far2[:2], far2[2:])):
        made = for_both(*part)
        two = (made, from_core(made, {b: b ^ 2 for b in index}))
        kept, sent = pair(own, two, 2 * n * cut)
        more = across(sent, [(b, h, h ^ 2) for b in index for h in (b, b ^ 2)])
        total = add((kept, more), part=1, parts=2)
        back = give_back(total, [(b, b ^ 2) for b in index])
        pieces += [kept, more, back]

    last = []
    for n, part in enumerate(far3):
        parts = 1 if n == 0 else 2
        made = pl.pallas_call(
            end_kernel,
            out_shape=[pltpu.VMEM((2 * tok_rows // parts, cut), jnp.bfloat16)] * parts,
            compiler_params=limit(12),
            cost_estimate=cost(8 * tok_rows * cut * wide, 8),
        )(gated, other, *turned, *part)
        last += [made[0], across(made[0], [(b, f ^ 2, f) for b, f in ends.items()])]
        if parts == 1:
            total = add(tuple(last), part=1, parts=2)
            last.append(give_back(total, ends.items()))
        else:
            pairs = [((g, b, f ^ 2), (1 - g, b, f)) for g in range(2) for b, f in ends.items()]
            last += [anywhere(made[1], pairs), give_back(made[1], ends.items())]

    sizes = {"width": wide * count, "count": count}
    most = pl.pallas_call(
        functools.partial(most_kernel, **sizes),
        in_specs=[SMEM, pl.BlockSpec(), pl.BlockSpec()] + [ANY] * 16,
        out_shape=table((tok_rows, 2 * half), jnp.bfloat16),
        scratch_shapes=[
            pltpu.VMEM((2 * tok_rows, half), jnp.bfloat16),
            pltpu.VMEM((2 * tok_rows, half), jnp.bfloat16),
            pltpu.SemaphoreType.DMA((7,)),
        ],
        compiler_params=limit(8),
    )(
        where, squares, squares_more, *pieces,
        near_kept, near_more, near_back, *last[:7],
    )
    return pl.pallas_call(
        functools.partial(last_kernel, **sizes),
        in_specs=[SMEM] + [pl.BlockSpec()] * 6 + [HBM],
        out_specs=HBM,
        out_shape=table((tok_rows, 2 * half), jnp.bfloat16),
        scratch_shapes=[
            pltpu.VMEM((tok_rows, cut), jnp.bfloat16),
            pltpu.VMEM((tok_rows, cut), jnp.bfloat16),
            pltpu.SemaphoreType.DMA((2,)),
        ],
        input_output_aliases={7: 0},
        compiler_params=limit(4),
    )(where, squares, squares_more, *last[7:], most)


def shards_general(
    layer_queries,
    layer_keys,
    layer_values,
    gate_logits,
    norm_gain,
    decay_exponents,
    doc_lengths,
    out_weight,
):
    tok_rows = layer_queries.shape[0]
    decay_rate, block_state, intra, cross = attention_parts(
        layer_queries, layer_keys, layer_values, decay_exponents, doc_lengths
    )
    count, block = lax.axis_size("seq"), lax.axis_index("seq")
    states = lax.all_gather(block_state, "seq")

    def turn(position, running):
        carry = carry_of(position, decay_rate, doc_lengths, tok_rows)
        longer = carry[:, None, None] * running + states[position]
        return jnp.where(position < block, longer, running)

    incoming = lax.fori_loop(0, count - 1, turn, jnp.zeros_like(block_state))
    attention = (intra() + cross(incoming)).reshape(layer_queries.shape)
    squares = lax.psum(jnp.sum(attention * attention, axis=1), "head")
    width_all = layer_queries.shape[1] * lax.axis_size("head")
    inv_scale = lax.rsqrt(squares / width_all + 1e-06)
    gated_out = (
        attention
        * inv_scale[:, None]
        * norm_gain.astype(jnp.float32)
        * jax.nn.sigmoid(gate_logits.astype(jnp.float32))
    ).astype(jnp.bfloat16)
    partials = lax.dot_general(
        gated_out,
        lax.all_gather(out_weight, "seq", axis=0, tiled=True),
        NT,
        preferred_element_type=jnp.float32,
    )
    return lax.psum_scatter(partials, "head", scatter_dimension=1, tiled=True).astype(jnp.bfloat16)


def solution(mesh):
    in_specs = (
        P(("groups", "seq"), "head"),
        P(("groups", "seq"), "head"),
        P(("groups", "seq"), "head"),
        P(("groups", "seq"), "head"),
        P("head"),
        P("head"),
        P("groups"),
        P("seq", "head"),
    )
    out_specs = P(("groups", "seq"), "head")
    seq, head = mesh.shape["seq"], mesh.shape["head"]
    grid = seq == head == 4 and mesh.shape["groups"] == 2
    shards = shards_grid if grid else shards_general
    return jax.shard_map(shards, mesh=mesh, in_specs=in_specs, out_specs=out_specs, check_vma=False)
```

```python
import functools

import jax
import jax.numpy as jnp
from jax import lax
from jax.experimental import pallas as pl
from jax.experimental.pallas import tpu as pltpu
from jax.sharding import PartitionSpec as P

HEAD_DIM = 128
NT = (((1,), (1,)), ((), ()))
TN = (((0,), (0,)), ((), ()))
SMEM = pl.BlockSpec(memory_space=pltpu.SMEM)
HBM = pl.BlockSpec(memory_space=pltpu.HBM)
ANY = pl.BlockSpec(memory_space=pl.ANY)
STEPS = 4


def cost(flops, mib):
    return pl.CostEstimate(flops=int(flops), bytes_accessed=int(mib * (1 << 20)), transcendentals=0)


def begin_of(doc_lengths, position):
    count = doc_lengths.shape[0]
    order = jnp.arange(count, dtype=jnp.int32)
    ends = jnp.sum(jnp.where(order[None, :] <= order[:, None], doc_lengths[None, :], 0), axis=1)
    return jnp.sum(jnp.where(ends[None, :] <= position[:, None], doc_lengths[None, :], 0), axis=1)


def attention_parts(layer_queries, layer_keys, layer_values, decay_exponents, doc_lengths):
    tok_rows = layer_queries.shape[0]
    heads_here = decay_exponents.shape[0]
    token_span = tok_rows * lax.axis_size("seq")
    block = lax.axis_index("seq")
    decay_rate = jnp.minimum(jnp.exp2(decay_exponents.astype(jnp.float32)) / token_span, 1.0 / 32.0)
    local_pos = jnp.arange(tok_rows, dtype=jnp.int32)
    position = block * tok_rows + local_pos
    within = position - begin_of(doc_lengths, position)
    query_heads = layer_queries.reshape(tok_rows, heads_here, HEAD_DIM)
    key_heads = layer_keys.reshape(tok_rows, heads_here, HEAD_DIM)
    value_heads = layer_values.reshape(tok_rows, heads_here, HEAD_DIM)

    last_within = within[tok_rows - 1]
    key_weight = jnp.where(
        (local_pos >= tok_rows - 1 - last_within)[:, None],
        jnp.exp(-decay_rate[None, :] * (tok_rows - local_pos)[:, None].astype(jnp.float32)),
        0.0,
    )
    scaled = (key_heads.astype(jnp.float32) * key_weight[:, :, None]).astype(jnp.bfloat16)
    block_state = jnp.einsum(
        "thd,the->hde", scaled, value_heads, preferred_element_type=jnp.float32
    )

    def intra():
        lag_grid = local_pos[:, None] - local_pos[None, :]
        valid_mask = (lag_grid >= 0) & (lag_grid <= within[:, None])
        decay_grid = jnp.where(
            valid_mask[None],
            jnp.exp(-decay_rate[:, None, None] * lag_grid[None].astype(jnp.float32)),
            0.0,
        )
        scores = jnp.einsum(
            "thd,shd->hts", query_heads, key_heads, preferred_element_type=jnp.float32
        )
        weights = (scores * decay_grid).astype(jnp.bfloat16)
        return jnp.einsum("hts,shd->thd", weights, value_heads, preferred_element_type=jnp.float32)

    def cross(incoming):
        query_weight = jnp.where(
            (within >= local_pos + 1)[:, None],
            jnp.exp(-decay_rate[None, :] * local_pos[:, None].astype(jnp.float32)),
            0.0,
        )
        return (
            jnp.einsum(
                "thd,hde->the",
                query_heads,
                incoming.astype(jnp.bfloat16),
                preferred_element_type=jnp.float32,
            )
            * query_weight[:, :, None]
        )

    return decay_rate, block_state, intra, cross


def carry_of(block, decay_rate, doc_lengths, tok_rows):
    last = (block * tok_rows + tok_rows - 1)[None]
    last_within = (last - begin_of(doc_lengths, last))[0]
    return jnp.where(last_within >= tok_rows, jnp.exp(-decay_rate * tok_rows), 0.0)


def limit(mib):
    return pltpu.CompilerParams(vmem_limit_bytes=mib << 20)


def begin_at(docs, position):
    begin, end = 0, 0
    for doc in range(docs.shape[0]):
        end = end + docs[doc]
        begin = jnp.where(position >= end, end, begin)
    return begin


def row_begin(docs, block, rows):
    shape = (rows, HEAD_DIM)
    position = block * rows + lax.broadcasted_iota(jnp.int32, shape, 0)
    begin = jnp.zeros(shape, jnp.int32)
    end = 0
    for doc in range(docs.shape[0]):
        end = end + docs[doc]
        begin = jnp.where(position >= end, end, begin)
    return begin - block * rows


def rate_of(exponents, head, span):
    doubled = lax.shift_left(jnp.int32(1), exponents[head]).astype(jnp.float32)
    return jnp.minimum(doubled * (1.0 / span), 1.0 / 32.0)


def each_head(width):
    here = width // HEAD_DIM
    for n in range(here):
        yield n, pl.program_id(0) * here + n, slice(n * HEAD_DIM, (n + 1) * HEAD_DIM)


def state_kernel(where, docs, exponents, keys, values, state, *, span):
    rows, width = keys.shape
    block = where[0]
    begin = begin_at(docs, block * rows + rows - 1)
    local = lax.broadcasted_iota(jnp.int32, (rows, HEAD_DIM), 0)
    kept = local >= begin - block * rows
    left = (rows - local).astype(jnp.float32)
    for n, head, columns in each_head(width):
        weight = jnp.where(kept, jnp.exp(-rate_of(exponents, head, span) * left), 0.0)
        scaled = (keys[:, columns].astype(jnp.float32) * weight).astype(jnp.bfloat16)
        made = lax.dot_general(scaled, values[:, columns], TN, preferred_element_type=jnp.float32)
        state[n] = made.astype(jnp.bfloat16)


def intra_kernel(where, docs, exponents, queries, keys, values, out, *, span):
    rows, width = queries.shape
    part = rows // 2
    begin = row_begin(docs, where[0], rows)[:, :1]
    for step in range(2):
        low, seen = step * part, (step + 1) * part
        row = low + lax.broadcasted_iota(jnp.int32, (part, seen), 0)
        column = lax.broadcasted_iota(jnp.int32, (part, seen), 1)
        valid = (column <= row) & (column >= begin[low:seen])
        lag = (row - column).astype(jnp.float32)
        for n, head, columns in each_head(width):
            scores = lax.dot_general(
                queries[low:seen, columns], keys[:seen, columns], NT, preferred_element_type=jnp.float32
            )
            decay = jnp.exp(-rate_of(exponents, head, span) * lag)
            weights = jnp.where(valid, scores * decay, 0.0).astype(jnp.bfloat16)
            out[low:seen, columns] = jnp.dot(
                weights, values[:seen, columns], preferred_element_type=jnp.float32
            )


def gate_kernel(
    where, docs, exponents, queries, intra, near, far, gain, gate, out, squares, total, *, span
):
    rows, width = queries.shape
    block = where[0]
    local = lax.broadcasted_iota(jnp.int32, (rows, HEAD_DIM), 0).astype(jnp.float32)
    reaches = row_begin(docs, block, rows) < 0
    whole = begin_at(docs, block * rows - 1) <= (block - 1) * rows - 1

    @pl.when(pl.program_id(0) == 0)
    def _():
        total[...] = jnp.zeros_like(total)

    for n, head, columns in each_head(width):
        rate = rate_of(exponents, head, span)
        weight = jnp.where(reaches, jnp.exp(-rate * local), 0.0)
        carry = jnp.exp(jnp.full((1, HEAD_DIM), -rate * rows, jnp.float32))
        carry = jnp.where(whole, carry, 0.0)
        incoming = near[n].astype(jnp.float32) + carry * far[n].astype(jnp.float32)
        cross = jnp.dot(
            queries[:, columns], incoming.astype(jnp.bfloat16), preferred_element_type=jnp.float32
        )
        attention = intra[:, columns] + cross * weight
        opened = jax.nn.sigmoid(gate[:, columns].astype(jnp.float32))
        out[:, columns] = (attention * gain[:, columns].astype(jnp.float32) * opened).astype(
            jnp.bfloat16
        )
        total[...] += attention * attention

    @pl.when(pl.program_id(0) == pl.num_programs(0) - 1)
    def _():
        squares[...] = lax.dot_general(
            jnp.ones((8, HEAD_DIM), jnp.float32),
            total[...],
            NT,
            precision=lax.Precision.HIGHEST,
            preferred_element_type=jnp.float32,
        )


def product_kernel(*refs, lefts, weights, tile, plan):
    out, stream, sems = refs[lefts + weights :]
    copies, place = [], 0
    for n in range(weights):
        weight = refs[lefts + n]
        for start in range(0, weight.shape[0], tile):
            copies.append(
                pltpu.make_async_copy(
                    weight.at[pl.ds(start, tile)], stream.at[pl.ds(place, tile)], sems.at[place // tile]
                )
            )
            place += tile
    for copy in copies:
        copy.start()
    for first, rows, left, row, column in plan:
        left = refs[left]
        for start in range(first, first + rows, tile):
            if left is refs[0]:
                copies[start // tile].wait()
            made = lax.dot_general(
                left[...], stream[pl.ds(start, tile)], NT, preferred_element_type=jnp.float32
            )
            out[pl.ds(row, left.shape[0]), pl.ds(column + start - first, tile)] = made.astype(
                jnp.bfloat16
            )


def end_kernel(own, other, own_turned, other_turned, weight, weight_turned, *outs):
    rows = own.shape[0]
    places = outs if len(outs) == 2 else [outs[0].at[pl.ds(n * rows, rows)] for n in range(2)]
    for one, two, out in zip((own, other), (own_turned, other_turned), places):
        total = lax.dot_general(one[...], weight[...], NT, preferred_element_type=jnp.float32)
        total += lax.dot_general(
            two[...], weight_turned[...], NT, preferred_element_type=jnp.float32
        )
        out[...] = total.astype(jnp.bfloat16)


def added(one, two):
    return (one.astype(jnp.float32) + two.astype(jnp.float32)).astype(jnp.bfloat16)


def split_kernel(where, made, come, kept, sent):
    half = kept.shape[1]
    keeps_low = (where[2] ^ (where[0] - 1)) & 2 == 0
    total = added(made[...], come[...])
    for value, first, second in ((True, kept, sent), (False, sent, kept)):

        @pl.when(keeps_low == value)
        def _(first=first, second=second):
            first[...] = total[:, :half]
            second[...] = total[:, half:]


def pair_kernel(where, own, own_come, two, two_come, kept, sent):
    keeps_own = (where[2] ^ where[0]) & 2 == 0
    for value, first, second in ((True, kept, sent), (False, sent, kept)):

        @pl.when(keeps_own == value)
        def _(first=first, second=second):
            first[...] = added(own[...], own_come[...])
            second[...] = added(two[...], two_come[...])


def add_kernel(*refs):
    out, column = refs[-1], 0
    for one, two in zip(refs[:-1:2], refs[1::2]):
        here = one.shape[1]
        out[:, column : column + here] = added(one[...], two[...])
        column += here


def run(sems, *pairs):
    copies = [pltpu.make_async_copy(a, b, sems.at[n]) for n, (a, b) in enumerate(pairs)]
    for copy in copies:
        copy.start()
    for copy in copies:
        copy.wait()


def cut_kernel(where, weight, *refs, half):
    outs, sems = refs[:-1], refs[-1]
    at, pairs = 0, []
    for out in outs:
        start = pl.multiple_of(where[1] * half + at, 128)
        pairs.append((weight.at[pl.ds(start, out.shape[0])], out))
        at += out.shape[0]
    run(sems, *pairs)


def pick_kernel(where, low, high, *refs, upper, start):
    outs, sems = refs[:-1], refs[-1]
    for above, source, offset in ((True, low, 0), (False, high, start)):

        @pl.when((where[0] >= upper) == above)
        def _(source=source, offset=offset):
            pairs, at = [], offset
            for out in outs:
                pairs.append((source.at[pl.ds(at, out.shape[0])], out))
                at += out.shape[0]
            run(sems, *pairs)


def scale_of(squares, more, width):
    mean = jnp.transpose(squares[...] + more[...])[:, :1] / width
    return lax.rsqrt(mean + 1e-06)


def at_end(where, count):
    return ((where[0] == 0) | (where[0] == count - 1)) & (where[0] ^ where[2] == count - 1)


def most_kernel(
    where, squares, squares_more, kept_a, more_a, back_a, kept_b, more_b, back_b, near, near_more, near_back,
    end_a, end_a_more, end_a_back, end_b, end_b_more, end_b_across, end_b_back, out, one, two, sems,
    *, width, count
):
    rows, full = out.shape
    half = full // 2
    cut = end_a.shape[1]
    scale = scale_of(squares, squares_more, width)
    apart = where[0] ^ where[2]
    end = at_end(where, count)
    beside = (apart & 1 == 1) & ~end
    low, high = pl.ds(0, rows), pl.ds(rows, rows)
    first, second = pl.ds(0, cut), pl.ds(cut, cut)
    most, others = pl.ds(0, 2 * cut), pl.ds(2 * cut, half - 2 * cut)

    def put(start, *parts):
        total = sum(part.astype(jnp.float32) for part in parts)
        out[:, pl.ds(start, parts[0].shape[1])] = (total * scale).astype(jnp.bfloat16)

    @pl.when(apart == 0)
    def _():
        run(
            sems,
            (kept_a, one.at[:, most]),
            (more_a, two.at[:, most]),
            (kept_b, one.at[:, others]),
            (more_b, two.at[:, others]),
        )
        for side in range(2):
            span = pl.ds(side * rows, rows)
            put(side * half, one[span], two[span])

    @pl.when(apart == 2)
    def _():
        run(
            sems,
            (kept_a.at[low], one.at[low, most]),
            (more_a.at[low], two.at[low, most]),
            (kept_b.at[low], one.at[low, others]),
            (more_b.at[low], two.at[low, others]),
            (back_a, one.at[high, most]),
            (back_b, one.at[high, others]),
        )

    @pl.when(beside)
    def _():
        run(
            sems,
            (near.at[low], one.at[low]),
            (near_more.at[low], two.at[low]),
            (near_back, one.at[high]),
        )

    @pl.when(end)
    def _():
        run(
            sems,
            (end_a.at[low], one.at[low, first]),
            (end_b.at[low], one.at[low, second]),
            (end_a_more.at[low], two.at[low, first]),
            (end_b_more.at[low], two.at[low, second]),
            (end_a_back, one.at[high, first]),
            (end_b_across, one.at[high, second]),
            (end_b_back, two.at[high, second]),
        )

    for group in range(2):
        this = group * half

        @pl.when((apart > 0) & ~end & (where[1] == group))
        def _(this=this):
            put(this, one[low], two[low])
            put(half - this, one[high])

        @pl.when(end & (where[1] == group))
        def _(this=this):
            put(this, one[low, : 2 * cut], two[low, : 2 * cut])
            put(half - this, one[high, :cut])
            put(half - this + cut, one[high, cut : 2 * cut], two[high, cut : 2 * cut])


def last_kernel(
    where, squares, squares_more, kept, more, across, back, most, out, this, that, sems, *, width, count
):
    half, cut = out.shape[1] // 2, kept.shape[1]
    for group in range(2):

        @pl.when(at_end(where, count) & (where[1] == group))
        def _(group=group):
            scale = scale_of(squares, squares_more, width)
            for to, one, two in ((this, kept, more), (that, across, back)):
                total = one[...].astype(jnp.float32) + two[...].astype(jnp.float32)
                to[...] = (total * scale).astype(jnp.bfloat16)
            pairs = [
                (ref, out.at[:, pl.ds(side * half + half - cut, cut)])
                for ref, side in ((this, group), (that, 1 - group))
            ]
            run(sems, *pairs)


def shards_grid(
    layer_queries,
    layer_keys,
    layer_values,
    gate_logits,
    norm_gain,
    decay_exponents,
    doc_lengths,
    out_weight,
):
    count, group, block, head = (
        lax.axis_size("seq"),
        lax.axis_index("groups"),
        lax.axis_index("seq"),
        lax.axis_index("head"),
    )
    tok_rows, wide = layer_queries.shape
    heads_here = decay_exponents.shape[0]
    half = out_weight.shape[0] // 2
    cut = half // 3
    span = tok_rows * count
    index = range(count)
    table = jax.ShapeDtypeStruct

    def across(value, pairs):
        return lax.ppermute(
            value, ("seq", "head"), [(b * count + h, b * count + k) for b, h, k in pairs]
        )

    where = jnp.stack([block, group, head])

    up = [(i, i + 1) for i in range(count - 1)]
    down = [(i + 1, i) for i in range(count - 1)]
    held = pltpu.with_memory_space_constraint(out_weight, pltpu.HBM)

    def take(*sizes):
        return pl.pallas_call(
            functools.partial(cut_kernel, half=half),
            in_specs=[SMEM, HBM],
            out_shape=[pltpu.VMEM((rows, wide), jnp.bfloat16) for rows in sizes],
            scratch_shapes=[pltpu.SemaphoreType.DMA((len(sizes),))],
            compiler_params=limit(2),
        )(where, held)

    (mine,) = take(half)
    low_a, low_b = take(2 * cut, cut)
    low = [lax.ppermute(low_a, "seq", up), lax.ppermute(low_b, "seq", up)]
    high = lax.ppermute(mine, "seq", down)
    low2 = [lax.ppermute(low[n], "seq", up[1:]) for n in range(2)]
    high2 = lax.ppermute(high, "seq", down[:-1])

    def pick(part, start, outs):
        return pl.pallas_call(
            functools.partial(pick_kernel, upper=count // 2, start=start),
            in_specs=[SMEM, HBM, HBM],
            out_shape=[pltpu.VMEM((cut, wide), jnp.bfloat16)] * outs,
            scratch_shapes=[pltpu.SemaphoreType.DMA((outs,))],
            compiler_params=limit(2),
        )(where, part, high2)

    far2 = [*pick(low2[0], 0, 2), *pick(low2[1], 2 * cut, 1)]
    ends = {0: (count - 1, 1), count - 1: (0, count - 2)}
    far3 = []
    for part in far2:
        same, cross = (
            lax.ppermute(
                part,
                ("seq", "head"),
                [
                    (b * count + (h ^ turn), end * count + h)
                    for end, (f, b) in ends.items()
                    for h in index
                    if (h ^ f) & 1 == 0
                ],
            )
            for turn in (0, 1)
        )
        far3.append((same, cross))
    ends = {end: f for end, (f, _) in ends.items()}

    columns = pl.BlockSpec((tok_rows, wide // STEPS), lambda n: (0, n))
    square = pl.BlockSpec((heads_here // STEPS, HEAD_DIM, HEAD_DIM), lambda n: (n, 0, 0))
    state = pl.pallas_call(
        functools.partial(state_kernel, span=span),
        grid=(STEPS,),
        in_specs=[SMEM, SMEM, SMEM, columns, columns],
        out_specs=square,
        out_shape=table((heads_here, HEAD_DIM, HEAD_DIM), jnp.bfloat16),
        compiler_params=limit(8),
    )(where, doc_lengths, decay_exponents, layer_keys, layer_values)
    near_state = lax.ppermute(state, "seq", up)
    far_state = lax.ppermute(state, "seq", [(i, i + 2) for i in range(count - 2)])
    intra = pl.pallas_call(
        functools.partial(intra_kernel, span=span),
        grid=(STEPS,),
        in_specs=[SMEM, SMEM, SMEM, columns, columns, columns],
        out_specs=columns,
        out_shape=table((tok_rows, wide), jnp.float32),
        compiler_params=limit(12),
    )(where, doc_lengths, decay_exponents, layer_queries, layer_keys, layer_values)
    gated, squares = pl.pallas_call(
        functools.partial(gate_kernel, span=span),
        grid=(STEPS,),
        in_specs=[
            SMEM, SMEM, SMEM, columns, columns, square, square,
            pl.BlockSpec((1, wide // STEPS), lambda n: (0, n)), columns,
        ],
        out_specs=[columns, pl.BlockSpec((8, tok_rows), lambda n: (0, 0))],
        out_shape=[table((tok_rows, wide), jnp.bfloat16), table((8, tok_rows), jnp.float32)],
        scratch_shapes=[pltpu.VMEM((tok_rows, HEAD_DIM), jnp.float32)],
        compiler_params=limit(12),
    )(
        where, doc_lengths, decay_exponents, layer_queries, intra, near_state, far_state,
        norm_gain[None, :], gate_logits,
    )
    other = lax.ppermute(gated, "groups", [(0, 1), (1, 0)])
    turned = [
        across(value, [(b, h, h ^ 1) for b in index for h in index])
        for value in (gated, other)
    ]
    squares = squares + lax.ppermute(squares, "head", [(i, i ^ 1) for i in index])
    squares_more = lax.ppermute(squares, "head", [(i, i ^ 2) for i in index])

    def product(shape, lefts, weights, plan, space=ANY):
        total = sum(weight.shape[0] for weight in weights)
        tile = 256
        return pl.pallas_call(
            functools.partial(
                product_kernel, lefts=len(lefts), weights=len(weights), tile=tile, plan=plan
            ),
            in_specs=[pl.BlockSpec()] * len(lefts) + [space] * len(weights),
            out_shape=pltpu.VMEM(shape, jnp.bfloat16),
            scratch_shapes=[
                pltpu.VMEM((total, wide), jnp.bfloat16),
                pltpu.SemaphoreType.DMA((total // tile,)),
            ],
            compiler_params=limit(12),
            cost_estimate=cost(2 * shape[0] * shape[1] * wide, 8),
        )(*lefts, *weights)

    def for_both(*weights):
        plan, column = [], 0
        for weight in weights:
            rows = weight.shape[0]
            plan += [(column, rows, side, side * tok_rows, column) for side in range(2)]
            column += rows
        return product((2 * tok_rows, column), (gated, other), weights, plan)

    def split(made, come):
        rows = 2 * tok_rows // STEPS
        return pl.pallas_call(
            split_kernel,
            grid=(STEPS,),
            in_specs=[SMEM] + [pl.BlockSpec((rows, 2 * half), lambda n: (n, 0))] * 2,
            out_specs=[pl.BlockSpec((rows, half), lambda n: (n, 0))] * 2,
            out_shape=[pltpu.VMEM((2 * tok_rows, half), jnp.bfloat16)] * 2,
            compiler_params=limit(8),
            cost_estimate=cost(4 * tok_rows * half, 9),
        )(where, made, come)

    def pair(own, two, start):
        rows, width = two[0].shape
        size = (rows // 2, cut)
        shifted = pl.BlockSpec(size, lambda n, c: (n, c + start // cut))
        plain = pl.BlockSpec(size, lambda n, c: (n, c))
        return pl.pallas_call(
            pair_kernel,
            grid=(2, width // cut),
            in_specs=[SMEM, shifted, shifted, plain, plain],
            out_specs=[plain, plain],
            out_shape=[pltpu.VMEM((rows, width), jnp.bfloat16)] * 2,
            compiler_params=limit(8),
            cost_estimate=cost(rows * width, 6),
        )(where, *own, *two)

    def add(*pairs, part=0, parts=1):
        rows, width = pairs[0][0].shape[0] // parts, sum(one.shape[1] for one, _ in pairs)
        steps = 2
        operands = [value for pair in pairs for value in pair]

        def block(width, part=0):
            return pl.BlockSpec((rows // steps, width), lambda n: (part * steps + n, 0))

        return pl.pallas_call(
            add_kernel,
            grid=(steps,),
            in_specs=[block(value.shape[1], part) for value in operands],
            out_specs=block(width),
            out_shape=pltpu.VMEM((rows, width), jnp.bfloat16),
            compiler_params=limit(6),
            cost_estimate=cost(rows * width, 3),
        )(*operands)

    def from_core(made, wanted):
        pairs = [(b, h, h ^ 1) for b, f in wanted.items() for h in index if (h ^ f) & 1]
        return across(made, pairs)

    def anywhere(value, pairs):
        flat = [tuple((g * count + b) * count + h for g, b, h in pair) for pair in pairs]
        return lax.ppermute(value, ("groups", "seq", "head"), flat)

    def give_back(total, owners):
        return anywhere(total, [((g, b, f), (1 - g, b, f)) for g in range(2) for b, f in owners])

    plan = [(side * half, half, 0, side * tok_rows, 0) for side in range(2)]
    made = product((2 * tok_rows, half), (gated,), (held,), plan, HBM)
    own = (made, from_core(made, {b: b for b in index}))

    nears = [(b, f) for b in index for f in (b - 1, b + 1) if 0 <= f < count]
    made = for_both(*low, high)
    come = from_core(made, {b: f for b, f in nears})
    near_kept, near_sent = split(made, come)
    near_more = across(near_sent, [(b, f ^ 2, f) for b, f in nears])
    near_back = give_back(add((near_kept, near_more), part=1, parts=2), nears)

    pieces = []
    for n, part in enumerate((far2[:2], far2[2:])):
        made = for_both(*part)
        two = (made, from_core(made, {b: b ^ 2 for b in index}))
        kept, sent = pair(own, two, 2 * n * cut)
        more = across(sent, [(b, h, h ^ 2) for b in index for h in (b, b ^ 2)])
        total = add((kept, more), part=1, parts=2)
        back = give_back(total, [(b, b ^ 2) for b in index])
        pieces += [kept, more, back]

    last = []
    for n, part in enumerate(far3):
        parts = 1 if n == 0 else 2
        made = pl.pallas_call(
            end_kernel,
            out_shape=[pltpu.VMEM((2 * tok_rows // parts, cut), jnp.bfloat16)] * parts,
            compiler_params=limit(12),
            cost_estimate=cost(8 * tok_rows * cut * wide, 8),
        )(gated, other, *turned, *part)
        last += [made[0], across(made[0], [(b, f ^ 2, f) for b, f in ends.items()])]
        if parts == 1:
            total = add(tuple(last), part=1, parts=2)
            last.append(give_back(total, ends.items()))
        else:
            pairs = [((g, b, f ^ 2), (1 - g, b, f)) for g in range(2) for b, f in ends.items()]
            last += [anywhere(made[1], pairs), give_back(made[1], ends.items())]

    sizes = {"width": wide * count, "count": count}
    most = pl.pallas_call(
        functools.partial(most_kernel, **sizes),
        in_specs=[SMEM, pl.BlockSpec(), pl.BlockSpec()] + [ANY] * 16,
        out_shape=table((tok_rows, 2 * half), jnp.bfloat16),
        scratch_shapes=[
            pltpu.VMEM((2 * tok_rows, half), jnp.bfloat16),
            pltpu.VMEM((2 * tok_rows, half), jnp.bfloat16),
            pltpu.SemaphoreType.DMA((7,)),
        ],
        compiler_params=limit(8),
    )(
        where, squares, squares_more, *pieces,
        near_kept, near_more, near_back, *last[:7],
    )
    return pl.pallas_call(
        functools.partial(last_kernel, **sizes),
        in_specs=[SMEM] + [pl.BlockSpec()] * 6 + [HBM],
        out_specs=HBM,
        out_shape=table((tok_rows, 2 * half), jnp.bfloat16),
        scratch_shapes=[
            pltpu.VMEM((tok_rows, cut), jnp.bfloat16),
            pltpu.VMEM((tok_rows, cut), jnp.bfloat16),
            pltpu.SemaphoreType.DMA((2,)),
        ],
        input_output_aliases={7: 0},
        compiler_params=limit(4),
    )(where, squares, squares_more, *last[7:], most)


def shards_general(
    layer_queries,
    layer_keys,
    layer_values,
    gate_logits,
    norm_gain,
    decay_exponents,
    doc_lengths,
    out_weight,
):
    tok_rows = layer_queries.shape[0]
    decay_rate, block_state, intra, cross = attention_parts(
        layer_queries, layer_keys, layer_values, decay_exponents, doc_lengths
    )
    count, block = lax.axis_size("seq"), lax.axis_index("seq")
    states = lax.all_gather(block_state, "seq")

    def turn(position, running):
        carry = carry_of(position, decay_rate, doc_lengths, tok_rows)
        longer = carry[:, None, None] * running + states[position]
        return jnp.where(position < block, longer, running)

    incoming = lax.fori_loop(0, count - 1, turn, jnp.zeros_like(block_state))
    attention = (intra() + cross(incoming)).reshape(layer_queries.shape)
    squares = lax.psum(jnp.sum(attention * attention, axis=1), "head")
    width_all = layer_queries.shape[1] * lax.axis_size("head")
    inv_scale = lax.rsqrt(squares / width_all + 1e-06)
    gated_out = (
        attention
        * inv_scale[:, None]
        * norm_gain.astype(jnp.float32)
        * jax.nn.sigmoid(gate_logits.astype(jnp.float32))
    ).astype(jnp.bfloat16)
    partials = lax.dot_general(
        gated_out,
        lax.all_gather(out_weight, "seq", axis=0, tiled=True),
        NT,
        preferred_element_type=jnp.float32,
    )
    return lax.psum_scatter(partials, "head", scatter_dimension=1, tiled=True).astype(jnp.bfloat16)


def solution(mesh):
    in_specs = (
        P(("groups", "seq"), "head"),
        P(("groups", "seq"), "head"),
        P(("groups", "seq"), "head"),
        P(("groups", "seq"), "head"),
        P("head"),
        P("head"),
        P("groups"),
        P("seq", "head"),
    )
    out_specs = P(("groups", "seq"), "head")
    seq, head = mesh.shape["seq"], mesh.shape["head"]
    grid = seq == head == 4 and mesh.shape["groups"] == 2
    shards = shards_grid if grid else shards_general
    return jax.shard_map(shards, mesh=mesh, in_specs=in_specs, out_specs=out_specs, check_vma=False)
```

```python
import functools

import jax
import jax.numpy as jnp
from jax import lax
from jax.experimental import pallas as pl
from jax.experimental.pallas import tpu as pltpu
from jax.sharding import PartitionSpec as P

HEAD_DIM = 128
NT = (((1,), (1,)), ((), ()))
TN = (((0,), (0,)), ((), ()))
SMEM = pl.BlockSpec(memory_space=pltpu.SMEM)
HBM = pl.BlockSpec(memory_space=pltpu.HBM)
ANY = pl.BlockSpec(memory_space=pl.ANY)
STEPS = 4


def cost(flops, mib):
    return pl.CostEstimate(flops=int(flops), bytes_accessed=int(mib * (1 << 20)), transcendentals=0)


def begin_of(doc_lengths, position):
    count = doc_lengths.shape[0]
    order = jnp.arange(count, dtype=jnp.int32)
    ends = jnp.sum(jnp.where(order[None, :] <= order[:, None], doc_lengths[None, :], 0), axis=1)
    return jnp.sum(jnp.where(ends[None, :] <= position[:, None], doc_lengths[None, :], 0), axis=1)


def attention_parts(layer_queries, layer_keys, layer_values, decay_exponents, doc_lengths):
    tok_rows = layer_queries.shape[0]
    heads_here = decay_exponents.shape[0]
    token_span = tok_rows * lax.axis_size("seq")
    block = lax.axis_index("seq")
    decay_rate = jnp.minimum(jnp.exp2(decay_exponents.astype(jnp.float32)) / token_span, 1.0 / 32.0)
    local_pos = jnp.arange(tok_rows, dtype=jnp.int32)
    position = block * tok_rows + local_pos
    within = position - begin_of(doc_lengths, position)
    query_heads = layer_queries.reshape(tok_rows, heads_here, HEAD_DIM)
    key_heads = layer_keys.reshape(tok_rows, heads_here, HEAD_DIM)
    value_heads = layer_values.reshape(tok_rows, heads_here, HEAD_DIM)

    last_within = within[tok_rows - 1]
    key_weight = jnp.where(
        (local_pos >= tok_rows - 1 - last_within)[:, None],
        jnp.exp(-decay_rate[None, :] * (tok_rows - local_pos)[:, None].astype(jnp.float32)),
        0.0,
    )
    scaled = (key_heads.astype(jnp.float32) * key_weight[:, :, None]).astype(jnp.bfloat16)
    block_state = jnp.einsum(
        "thd,the->hde", scaled, value_heads, preferred_element_type=jnp.float32
    )

    def intra():
        lag_grid = local_pos[:, None] - local_pos[None, :]
        valid_mask = (lag_grid >= 0) & (lag_grid <= within[:, None])
        decay_grid = jnp.where(
            valid_mask[None],
            jnp.exp(-decay_rate[:, None, None] * lag_grid[None].astype(jnp.float32)),
            0.0,
        )
        scores = jnp.einsum(
            "thd,shd->hts", query_heads, key_heads, preferred_element_type=jnp.float32
        )
        weights = (scores * decay_grid).astype(jnp.bfloat16)
        return jnp.einsum("hts,shd->thd", weights, value_heads, preferred_element_type=jnp.float32)

    def cross(incoming):
        query_weight = jnp.where(
            (within >= local_pos + 1)[:, None],
            jnp.exp(-decay_rate[None, :] * local_pos[:, None].astype(jnp.float32)),
            0.0,
        )
        return (
            jnp.einsum(
                "thd,hde->the",
                query_heads,
                incoming.astype(jnp.bfloat16),
                preferred_element_type=jnp.float32,
            )
            * query_weight[:, :, None]
        )

    return decay_rate, block_state, intra, cross


def carry_of(block, decay_rate, doc_lengths, tok_rows):
    last = (block * tok_rows + tok_rows - 1)[None]
    last_within = (last - begin_of(doc_lengths, last))[0]
    return jnp.where(last_within >= tok_rows, jnp.exp(-decay_rate * tok_rows), 0.0)


def limit(mib):
    return pltpu.CompilerParams(vmem_limit_bytes=mib << 20)


def begin_at(docs, position):
    begin, end = 0, 0
    for doc in range(docs.shape[0]):
        end = end + docs[doc]
        begin = jnp.where(position >= end, end, begin)
    return begin


def row_begin(docs, block, rows):
    shape = (rows, HEAD_DIM)
    position = block * rows + lax.broadcasted_iota(jnp.int32, shape, 0)
    begin = jnp.zeros(shape, jnp.int32)
    end = 0
    for doc in range(docs.shape[0]):
        end = end + docs[doc]
        begin = jnp.where(position >= end, end, begin)
    return begin - block * rows


def rate_of(exponents, head, span):
    doubled = lax.shift_left(jnp.int32(1), exponents[head]).astype(jnp.float32)
    return jnp.minimum(doubled * (1.0 / span), 1.0 / 32.0)


def each_head(width):
    here = width // HEAD_DIM
    for n in range(here):
        yield n, pl.program_id(0) * here + n, slice(n * HEAD_DIM, (n + 1) * HEAD_DIM)


def state_kernel(where, docs, exponents, keys, values, state, *, span):
    rows, width = keys.shape
    block = where[0]
    begin = begin_at(docs, block * rows + rows - 1)
    local = lax.broadcasted_iota(jnp.int32, (rows, HEAD_DIM), 0)
    kept = local >= begin - block * rows
    left = (rows - local).astype(jnp.float32)
    for n, head, columns in each_head(width):
        weight = jnp.where(kept, jnp.exp(-rate_of(exponents, head, span) * left), 0.0)
        scaled = (keys[:, columns].astype(jnp.float32) * weight).astype(jnp.bfloat16)
        made = lax.dot_general(scaled, values[:, columns], TN, preferred_element_type=jnp.float32)
        state[n] = made.astype(jnp.bfloat16)


def intra_kernel(where, docs, exponents, queries, keys, values, out, *, span):
    rows, width = queries.shape
    part = rows // 2
    begin = row_begin(docs, where[0], rows)[:, :1]
    for step in range(2):
        low, seen = step * part, (step + 1) * part
        row = low + lax.broadcasted_iota(jnp.int32, (part, seen), 0)
        column = lax.broadcasted_iota(jnp.int32, (part, seen), 1)
        valid = (column <= row) & (column >= begin[low:seen])
        lag = (row - column).astype(jnp.float32)
        for n, head, columns in each_head(width):
            scores = lax.dot_general(
                queries[low:seen, columns], keys[:seen, columns], NT, preferred_element_type=jnp.float32
            )
            decay = jnp.exp(-rate_of(exponents, head, span) * lag)
            weights = jnp.where(valid, scores * decay, 0.0).astype(jnp.bfloat16)
            out[low:seen, columns] = jnp.dot(
                weights, values[:seen, columns], preferred_element_type=jnp.float32
            )


def gate_kernel(
    where, docs, exponents, queries, intra, near, far, gain, gate, out, squares, total, *, span
):
    rows, width = queries.shape
    block = where[0]
    local = lax.broadcasted_iota(jnp.int32, (rows, HEAD_DIM), 0).astype(jnp.float32)
    reaches = row_begin(docs, block, rows) < 0
    whole = begin_at(docs, block * rows - 1) <= (block - 1) * rows - 1

    @pl.when(pl.program_id(0) == 0)
    def _():
        total[...] = jnp.zeros_like(total)

    for n, head, columns in each_head(width):
        rate = rate_of(exponents, head, span)
        weight = jnp.where(reaches, jnp.exp(-rate * local), 0.0)
        carry = jnp.exp(jnp.full((1, HEAD_DIM), -rate * rows, jnp.float32))
        carry = jnp.where(whole, carry, 0.0)
        incoming = near[n].astype(jnp.float32) + carry * far[n].astype(jnp.float32)
        cross = jnp.dot(
            queries[:, columns], incoming.astype(jnp.bfloat16), preferred_element_type=jnp.float32
        )
        attention = intra[:, columns] + cross * weight
        opened = jax.nn.sigmoid(gate[:, columns].astype(jnp.float32))
        out[:, columns] = (attention * gain[:, columns].astype(jnp.float32) * opened).astype(
            jnp.bfloat16
        )
        total[...] += attention * attention

    @pl.when(pl.program_id(0) == pl.num_programs(0) - 1)
    def _():
        squares[...] = lax.dot_general(
            jnp.ones((8, HEAD_DIM), jnp.float32),
            total[...],
            NT,
            precision=lax.Precision.HIGHEST,
            preferred_element_type=jnp.float32,
        )


def product_kernel(*refs, lefts, weights, tile, plan):
    out, stream, sems = refs[lefts + weights :]
    copies, place = [], 0
    for n in range(weights):
        weight = refs[lefts + n]
        for start in range(0, weight.shape[0], tile):
            copies.append(
                pltpu.make_async_copy(
                    weight.at[pl.ds(start, tile)], stream.at[pl.ds(place, tile)], sems.at[place // tile]
                )
            )
            place += tile
    for copy in copies:
        copy.start()
    for first, rows, left, row, column in plan:
        left = refs[left]
        for start in range(first, first + rows, tile):
            if left is refs[0]:
                copies[start // tile].wait()
            made = lax.dot_general(
                left[...], stream[pl.ds(start, tile)], NT, preferred_element_type=jnp.float32
            )
            out[pl.ds(row, left.shape[0]), pl.ds(column + start - first, tile)] = made.astype(
                jnp.bfloat16
            )


def end_kernel(own, other, own_turned, other_turned, weight, weight_turned, *outs):
    rows = own.shape[0]
    places = outs if len(outs) == 2 else [outs[0].at[pl.ds(n * rows, rows)] for n in range(2)]
    for one, two, out in zip((own, other), (own_turned, other_turned), places):
        total = lax.dot_general(one[...], weight[...], NT, preferred_element_type=jnp.float32)
        total += lax.dot_general(
            two[...], weight_turned[...], NT, preferred_element_type=jnp.float32
        )
        out[...] = total.astype(jnp.bfloat16)


def added(one, two):
    return (one.astype(jnp.float32) + two.astype(jnp.float32)).astype(jnp.bfloat16)


def split_kernel(where, made, come, kept, sent):
    half = kept.shape[1]
    keeps_low = (where[2] ^ (where[0] - 1)) & 2 == 0
    total = added(made[...], come[...])
    for value, first, second in ((True, kept, sent), (False, sent, kept)):

        @pl.when(keeps_low == value)
        def _(first=first, second=second):
            first[...] = total[:, :half]
            second[...] = total[:, half:]


def pair_kernel(where, own, own_come, two, two_come, kept, sent):
    keeps_own = (where[2] ^ where[0]) & 2 == 0
    for value, first, second in ((True, kept, sent), (False, sent, kept)):

        @pl.when(keeps_own == value)
        def _(first=first, second=second):
            first[...] = added(own[...], own_come[...])
            second[...] = added(two[...], two_come[...])


def add_kernel(*refs):
    out, column = refs[-1], 0
    for one, two in zip(refs[:-1:2], refs[1::2]):
        here = one.shape[1]
        out[:, column : column + here] = added(one[...], two[...])
        column += here


def run(sems, *pairs):
    copies = [pltpu.make_async_copy(a, b, sems.at[n]) for n, (a, b) in enumerate(pairs)]
    for copy in copies:
        copy.start()
    for copy in copies:
        copy.wait()


def cut_kernel(where, weight, *refs, half):
    outs, sems = refs[:-1], refs[-1]
    at, pairs = 0, []
    for out in outs:
        start = pl.multiple_of(where[1] * half + at, 128)
        pairs.append((weight.at[pl.ds(start, out.shape[0])], out))
        at += out.shape[0]
    run(sems, *pairs)


def pick_kernel(where, low, high, *refs, upper, start):
    outs, sems = refs[:-1], refs[-1]
    for above, source, offset in ((True, low, 0), (False, high, start)):

        @pl.when((where[0] >= upper) == above)
        def _(source=source, offset=offset):
            pairs, at = [], offset
            for out in outs:
                pairs.append((source.at[pl.ds(at, out.shape[0])], out))
                at += out.shape[0]
            run(sems, *pairs)


def scale_of(squares, more, width):
    mean = jnp.transpose(squares[...] + more[...])[:, :1] / width
    return lax.rsqrt(mean + 1e-06)


def at_end(where, count):
    return ((where[0] == 0) | (where[0] == count - 1)) & (where[0] ^ where[2] == count - 1)


def most_kernel(
    where, squares, squares_more, kept_a, more_a, back_a, kept_b, more_b, back_b, near, near_more, near_back,
    end_a, end_a_more, end_a_back, end_b, end_b_more, end_b_across, end_b_back, out, one, two, sems,
    *, width, count
):
    rows, full = out.shape
    half = full // 2
    cut = end_a.shape[1]
    scale = scale_of(squares, squares_more, width)
    apart = where[0] ^ where[2]
    end = at_end(where, count)
    beside = (apart & 1 == 1) & ~end
    low, high = pl.ds(0, rows), pl.ds(rows, rows)
    first, second = pl.ds(0, cut), pl.ds(cut, cut)
    most, others = pl.ds(0, 2 * cut), pl.ds(2 * cut, half - 2 * cut)

    def put(start, *parts):
        total = sum(part.astype(jnp.float32) for part in parts)
        out[:, pl.ds(start, parts[0].shape[1])] = (total * scale).astype(jnp.bfloat16)

    @pl.when(apart == 0)
    def _():
        run(
            sems,
            (kept_a, one.at[:, most]),
            (more_a, two.at[:, most]),
            (kept_b, one.at[:, others]),
            (more_b, two.at[:, others]),
        )
        for side in range(2):
            span = pl.ds(side * rows, rows)
            put(side * half, one[span], two[span])

    @pl.when(apart == 2)
    def _():
        run(
            sems,
            (kept_a.at[low], one.at[low, most]),
            (more_a.at[low], two.at[low, most]),
            (kept_b.at[low], one.at[low, others]),
            (more_b.at[low], two.at[low, others]),
            (back_a, one.at[high, most]),
            (back_b, one.at[high, others]),
        )

    @pl.when(beside)
    def _():
        run(
            sems,
            (near.at[low], one.at[low]),
            (near_more.at[low], two.at[low]),
            (near_back, one.at[high]),
        )

    @pl.when(end)
    def _():
        run(
            sems,
            (end_a.at[low], one.at[low, first]),
            (end_b.at[low], one.at[low, second]),
            (end_a_more.at[low], two.at[low, first]),
            (end_b_more.at[low], two.at[low, second]),
            (end_a_back, one.at[high, first]),
            (end_b_across, one.at[high, second]),
            (end_b_back, two.at[high, second]),
        )

    for group in range(2):
        this = group * half

        @pl.when((apart > 0) & ~end & (where[1] == group))
        def _(this=this):
            put(this, one[low], two[low])
            put(half - this, one[high])

        @pl.when(end & (where[1] == group))
        def _(this=this):
            put(this, one[low, : 2 * cut], two[low, : 2 * cut])
            put(half - this, one[high, :cut])
            put(half - this + cut, one[high, cut : 2 * cut], two[high, cut : 2 * cut])


def last_kernel(
    where, squares, squares_more, kept, more, across, back, most, out, this, that, sems, *, width, count
):
    half, cut = out.shape[1] // 2, kept.shape[1]
    for group in range(2):

        @pl.when(at_end(where, count) & (where[1] == group))
        def _(group=group):
            scale = scale_of(squares, squares_more, width)
            copies = []
            for n, (to, side, one, two) in enumerate(
                ((this, group, kept, more), (that, 1 - group, across, back))
            ):
                total = one[...].astype(jnp.float32) + two[...].astype(jnp.float32)
                to[...] = (total * scale).astype(jnp.bfloat16)
                columns = pl.ds(side * half + half - cut, cut)
                copies.append(pltpu.make_async_copy(to, out.at[:, columns], sems.at[n]))
                copies[-1].start()
            for copy in copies:
                copy.wait()


def shards_grid(
    layer_queries,
    layer_keys,
    layer_values,
    gate_logits,
    norm_gain,
    decay_exponents,
    doc_lengths,
    out_weight,
):
    count, group, block, head = (
        lax.axis_size("seq"),
        lax.axis_index("groups"),
        lax.axis_index("seq"),
        lax.axis_index("head"),
    )
    tok_rows, wide = layer_queries.shape
    heads_here = decay_exponents.shape[0]
    half = out_weight.shape[0] // 2
    cut = half // 3
    span = tok_rows * count
    index = range(count)
    table = jax.ShapeDtypeStruct

    def across(value, pairs):
        return lax.ppermute(
            value, ("seq", "head"), [(b * count + h, b * count + k) for b, h, k in pairs]
        )

    where = jnp.stack([block, group, head])

    up = [(i, i + 1) for i in range(count - 1)]
    down = [(i + 1, i) for i in range(count - 1)]
    held = pltpu.with_memory_space_constraint(out_weight, pltpu.HBM)

    def take(*sizes):
        return pl.pallas_call(
            functools.partial(cut_kernel, half=half),
            in_specs=[SMEM, HBM],
            out_shape=[pltpu.VMEM((rows, wide), jnp.bfloat16) for rows in sizes],
            scratch_shapes=[pltpu.SemaphoreType.DMA((len(sizes),))],
            compiler_params=limit(2),
        )(where, held)

    (mine,) = take(half)
    low_a, low_b = take(2 * cut, cut)
    low = [lax.ppermute(low_a, "seq", up), lax.ppermute(low_b, "seq", up)]
    high = lax.ppermute(mine, "seq", down)
    low2 = [lax.ppermute(low[n], "seq", up[1:]) for n in range(2)]
    high2 = lax.ppermute(high, "seq", down[:-1])

    def pick(part, start, outs):
        return pl.pallas_call(
            functools.partial(pick_kernel, upper=count // 2, start=start),
            in_specs=[SMEM, HBM, HBM],
            out_shape=[pltpu.VMEM((cut, wide), jnp.bfloat16)] * outs,
            scratch_shapes=[pltpu.SemaphoreType.DMA((outs,))],
            compiler_params=limit(2),
        )(where, part, high2)

    far2 = [*pick(low2[0], 0, 2), *pick(low2[1], 2 * cut, 1)]
    ends = {0: (count - 1, 1), count - 1: (0, count - 2)}
    far3 = []
    for part in far2:
        same, cross = (
            lax.ppermute(
                part,
                ("seq", "head"),
                [
                    (b * count + (h ^ turn), end * count + h)
                    for end, (f, b) in ends.items()
                    for h in index
                    if (h ^ f) & 1 == 0
                ],
            )
            for turn in (0, 1)
        )
        far3.append((same, cross))
    ends = {end: f for end, (f, _) in ends.items()}

    columns = pl.BlockSpec((tok_rows, wide // STEPS), lambda n: (0, n))
    square = pl.BlockSpec((heads_here // STEPS, HEAD_DIM, HEAD_DIM), lambda n: (n, 0, 0))
    state = pl.pallas_call(
        functools.partial(state_kernel, span=span),
        grid=(STEPS,),
        in_specs=[SMEM, SMEM, SMEM, columns, columns],
        out_specs=square,
        out_shape=table((heads_here, HEAD_DIM, HEAD_DIM), jnp.bfloat16),
        compiler_params=limit(8),
    )(where, doc_lengths, decay_exponents, layer_keys, layer_values)
    near_state = lax.ppermute(state, "seq", up)
    far_state = lax.ppermute(state, "seq", [(i, i + 2) for i in range(count - 2)])
    intra = pl.pallas_call(
        functools.partial(intra_kernel, span=span),
        grid=(STEPS,),
        in_specs=[SMEM, SMEM, SMEM, columns, columns, columns],
        out_specs=columns,
        out_shape=table((tok_rows, wide), jnp.float32),
        compiler_params=limit(12),
    )(where, doc_lengths, decay_exponents, layer_queries, layer_keys, layer_values)
    gated, squares = pl.pallas_call(
        functools.partial(gate_kernel, span=span),
        grid=(STEPS,),
        in_specs=[
            SMEM, SMEM, SMEM, columns, columns, square, square,
            pl.BlockSpec((1, wide // STEPS), lambda n: (0, n)), columns,
        ],
        out_specs=[columns, pl.BlockSpec((8, tok_rows), lambda n: (0, 0))],
        out_shape=[table((tok_rows, wide), jnp.bfloat16), table((8, tok_rows), jnp.float32)],
        scratch_shapes=[pltpu.VMEM((tok_rows, HEAD_DIM), jnp.float32)],
        compiler_params=limit(12),
    )(
        where, doc_lengths, decay_exponents, layer_queries, intra, near_state, far_state,
        norm_gain[None, :], gate_logits,
    )
    other = lax.ppermute(gated, "groups", [(0, 1), (1, 0)])
    turned = [
        across(value, [(b, h, h ^ 1) for b in index for h in index])
        for value in (gated, other)
    ]
    squares = squares + lax.ppermute(squares, "head", [(i, i ^ 1) for i in index])
    squares_more = lax.ppermute(squares, "head", [(i, i ^ 2) for i in index])

    def product(shape, lefts, weights, plan, space=ANY):
        total = sum(weight.shape[0] for weight in weights)
        tile = 256
        return pl.pallas_call(
            functools.partial(
                product_kernel, lefts=len(lefts), weights=len(weights), tile=tile, plan=plan
            ),
            in_specs=[pl.BlockSpec()] * len(lefts) + [space] * len(weights),
            out_shape=pltpu.VMEM(shape, jnp.bfloat16),
            scratch_shapes=[
                pltpu.VMEM((total, wide), jnp.bfloat16),
                pltpu.SemaphoreType.DMA((total // tile,)),
            ],
            compiler_params=limit(12),
            cost_estimate=cost(2 * shape[0] * shape[1] * wide, 8),
        )(*lefts, *weights)

    def for_both(*weights):
        plan, column = [], 0
        for weight in weights:
            rows = weight.shape[0]
            plan += [(column, rows, side, side * tok_rows, column) for side in range(2)]
            column += rows
        return product((2 * tok_rows, column), (gated, other), weights, plan)

    def split(made, come):
        rows = 2 * tok_rows // STEPS
        return pl.pallas_call(
            split_kernel,
            grid=(STEPS,),
            in_specs=[SMEM] + [pl.BlockSpec((rows, 2 * half), lambda n: (n, 0))] * 2,
            out_specs=[pl.BlockSpec((rows, half), lambda n: (n, 0))] * 2,
            out_shape=[pltpu.VMEM((2 * tok_rows, half), jnp.bfloat16)] * 2,
            compiler_params=limit(8),
            cost_estimate=cost(4 * tok_rows * half, 9),
        )(where, made, come)

    def pair(own, two, start):
        rows, width = two[0].shape
        size = (rows // 2, cut)
        shifted = pl.BlockSpec(size, lambda n, c: (n, c + start // cut))
        plain = pl.BlockSpec(size, lambda n, c: (n, c))
        return pl.pallas_call(
            pair_kernel,
            grid=(2, width // cut),
            in_specs=[SMEM, shifted, shifted, plain, plain],
            out_specs=[plain, plain],
            out_shape=[pltpu.VMEM((rows, width), jnp.bfloat16)] * 2,
            compiler_params=limit(8),
            cost_estimate=cost(rows * width, 6),
        )(where, *own, *two)

    def add(*pairs, part=0, parts=1):
        rows, width = pairs[0][0].shape[0] // parts, sum(one.shape[1] for one, _ in pairs)
        steps = 2
        operands = [value for pair in pairs for value in pair]

        def block(width, part=0):
            return pl.BlockSpec((rows // steps, width), lambda n: (part * steps + n, 0))

        return pl.pallas_call(
            add_kernel,
            grid=(steps,),
            in_specs=[block(value.shape[1], part) for value in operands],
            out_specs=block(width),
            out_shape=pltpu.VMEM((rows, width), jnp.bfloat16),
            compiler_params=limit(6),
            cost_estimate=cost(rows * width, 3),
        )(*operands)

    def from_core(made, wanted):
        pairs = [(b, h, h ^ 1) for b, f in wanted.items() for h in index if (h ^ f) & 1]
        return across(made, pairs)

    def anywhere(value, pairs):
        flat = [tuple((g * count + b) * count + h for g, b, h in pair) for pair in pairs]
        return lax.ppermute(value, ("groups", "seq", "head"), flat)

    def give_back(total, owners):
        return anywhere(total, [((g, b, f), (1 - g, b, f)) for g in range(2) for b, f in owners])

    plan = [(side * half, half, 0, side * tok_rows, 0) for side in range(2)]
    made = product((2 * tok_rows, half), (gated,), (held,), plan, HBM)
    own = (made, from_core(made, {b: b for b in index}))

    nears = [(b, f) for b in index for f in (b - 1, b + 1) if 0 <= f < count]
    made = for_both(*low, high)
    come = from_core(made, {b: f for b, f in nears})
    near_kept, near_sent = split(made, come)
    near_more = across(near_sent, [(b, f ^ 2, f) for b, f in nears])
    near_back = give_back(add((near_kept, near_more), part=1, parts=2), nears)

    pieces = []
    for n, part in enumerate((far2[:2], far2[2:])):
        made = for_both(*part)
        two = (made, from_core(made, {b: b ^ 2 for b in index}))
        kept, sent = pair(own, two, 2 * n * cut)
        more = across(sent, [(b, h, h ^ 2) for b in index for h in (b, b ^ 2)])
        total = add((kept, more), part=1, parts=2)
        back = give_back(total, [(b, b ^ 2) for b in index])
        pieces += [kept, more, back]

    last = []
    for n, part in enumerate(far3):
        parts = 1 if n == 0 else 2
        made = pl.pallas_call(
            end_kernel,
            out_shape=[pltpu.VMEM((2 * tok_rows // parts, cut), jnp.bfloat16)] * parts,
            compiler_params=limit(12),
            cost_estimate=cost(8 * tok_rows * cut * wide, 8),
        )(gated, other, *turned, *part)
        last += [made[0], across(made[0], [(b, f ^ 2, f) for b, f in ends.items()])]
        if parts == 1:
            total = add(tuple(last), part=1, parts=2)
            last.append(give_back(total, ends.items()))
        else:
            pairs = [((g, b, f ^ 2), (1 - g, b, f)) for g in range(2) for b, f in ends.items()]
            last += [anywhere(made[1], pairs), give_back(made[1], ends.items())]

    sizes = {"width": wide * count, "count": count}
    most = pl.pallas_call(
        functools.partial(most_kernel, **sizes),
        in_specs=[SMEM, pl.BlockSpec(), pl.BlockSpec()] + [ANY] * 16,
        out_shape=table((tok_rows, 2 * half), jnp.bfloat16),
        scratch_shapes=[
            pltpu.VMEM((2 * tok_rows, half), jnp.bfloat16),
            pltpu.VMEM((2 * tok_rows, half), jnp.bfloat16),
            pltpu.SemaphoreType.DMA((7,)),
        ],
        compiler_params=limit(8),
    )(
        where, squares, squares_more, *pieces,
        near_kept, near_more, near_back, *last[:7],
    )
    return pl.pallas_call(
        functools.partial(last_kernel, **sizes),
        in_specs=[SMEM] + [pl.BlockSpec()] * 6 + [HBM],
        out_specs=HBM,
        out_shape=table((tok_rows, 2 * half), jnp.bfloat16),
        scratch_shapes=[
            pltpu.VMEM((tok_rows, cut), jnp.bfloat16),
            pltpu.VMEM((tok_rows, cut), jnp.bfloat16),
            pltpu.SemaphoreType.DMA((2,)),
        ],
        input_output_aliases={7: 0},
        compiler_params=limit(4),
    )(where, squares, squares_more, *last[7:], most)


def shards_general(
    layer_queries,
    layer_keys,
    layer_values,
    gate_logits,
    norm_gain,
    decay_exponents,
    doc_lengths,
    out_weight,
):
    tok_rows = layer_queries.shape[0]
    decay_rate, block_state, intra, cross = attention_parts(
        layer_queries, layer_keys, layer_values, decay_exponents, doc_lengths
    )
    count, block = lax.axis_size("seq"), lax.axis_index("seq")
    states = lax.all_gather(block_state, "seq")

    def turn(position, running):
        carry = carry_of(position, decay_rate, doc_lengths, tok_rows)
        longer = carry[:, None, None] * running + states[position]
        return jnp.where(position < block, longer, running)

    incoming = lax.fori_loop(0, count - 1, turn, jnp.zeros_like(block_state))
    attention = (intra() + cross(incoming)).reshape(layer_queries.shape)
    squares = lax.psum(jnp.sum(attention * attention, axis=1), "head")
    width_all = layer_queries.shape[1] * lax.axis_size("head")
    inv_scale = lax.rsqrt(squares / width_all + 1e-06)
    gated_out = (
        attention
        * inv_scale[:, None]
        * norm_gain.astype(jnp.float32)
        * jax.nn.sigmoid(gate_logits.astype(jnp.float32))
    ).astype(jnp.bfloat16)
    partials = lax.dot_general(
        gated_out,
        lax.all_gather(out_weight, "seq", axis=0, tiled=True),
        NT,
        preferred_element_type=jnp.float32,
    )
    return lax.psum_scatter(partials, "head", scatter_dimension=1, tiled=True).astype(jnp.bfloat16)


def solution(mesh):
    in_specs = (
        P(("groups", "seq"), "head"),
        P(("groups", "seq"), "head"),
        P(("groups", "seq"), "head"),
        P(("groups", "seq"), "head"),
        P("head"),
        P("head"),
        P("groups"),
        P("seq", "head"),
    )
    out_specs = P(("groups", "seq"), "head")
    seq, head = mesh.shape["seq"], mesh.shape["head"]
    grid = seq == head == 4 and mesh.shape["groups"] == 2
    shards = shards_grid if grid else shards_general
    return jax.shard_map(shards, mesh=mesh, in_specs=in_specs, out_specs=out_specs, check_vma=False)
```
